32 devices in a mesh: tm: 2 (over core), tile: 16 (over z, y, x).
Axes of the slice: x: 2, y: 2, z: 4, core: 2. Of those that a mesh axis runs over, the one named last changes fastest.
Arguments:
- features: bfloat16 [1, 8, 64, 64, 192], P(None, 'tm', 'tile'), may hold values from -60 to 60
- gain_one: float32 [192], replicated, may hold values from 0.5 to 1.5
- shift_one: float32 [192], replicated, may hold values from -3 to 3
- kernel_one: bfloat16 [3, 3, 3, 192, 192], replicated, may hold values from -0.078125 to 0.078125
- bias_one: float32 [192], replicated, may hold values from -3 to 3
- gain_two: float32 [192], replicated, may hold values from 0.5 to 1.5
- shift_two: float32 [192], replicated, may hold values from -3 to 3
- kernel_two: bfloat16 [3, 3, 3, 192, 192], replicated, may hold values from -0.078125 to 0.078125
- bias_two: float32 [192], replicated, may hold values from -3 to 3
- up_kernel: bfloat16 [3, 3, 192, 96], replicated, may hold values from -0.15625 to 0.15625
- up_bias: float32 [96], replicated, may hold values from -3 to 3
Outputs:
- decoded: bfloat16 [1, 8, 128, 64, 192], P(None, 'tm', 'tile')
The draws below stay inside these ranges and needn't reach their ends.
All inputs are finite; a program needn't handle non-finite values.
Results may differ from the reference program's by a relative error of at most 0.009.
Values may be sent and summed in bfloat16 or wider, within the bound.
A program may use at most 128 MiB of HBM per device.

```python
import jax
import jax.numpy as jnp
from jax import lax

C = 192
C2 = 96
G = 32
CLIPS = 1
W = 64
FRAMES = 8
H = 64


def draw_features(key, part):
    noise_key, row_key, col_key = jax.random.split(key, 3)
    shape_all = (CLIPS, FRAMES, H, W, C)
    row_place = jnp.arange(H, dtype=jnp.float32) / max(H - 1, 1)
    row_scale = 10.0 ** (jax.random.uniform(row_key, (H,), jnp.float32) - 0.5) * 3.0 ** (row_place - 1.0)
    col_scale = 10.0 ** (jax.random.uniform(col_key, (W,), jnp.float32) - 0.5)
    noise_draw = jax.random.truncated_normal(noise_key, -6.0, 6.0, shape_all, jnp.float32)
    scaled = noise_draw * row_scale[None, None, :, None, None] * col_scale[None, None, None, :, None]
    return scaled.astype(jnp.bfloat16)


def noise(rng, shape, width, most, held_as=jnp.bfloat16):
    drawn = width * jax.random.normal(rng, shape, jnp.float32)
    return jnp.clip(drawn, min=-most, max=most).astype(held_as)


def setup_inputs(seed: int = 0) -> dict:
    streams_of = jax.random.split(jax.random.key(seed), 12)
    features = draw_features(jax.random.fold_in(streams_of[11], 71), 0)
    gain_one = jnp.clip(1.0 + 0.1 * jax.random.normal(streams_of[1], (C,), jnp.float32), 0.5, 1.5)
    shift_one = noise(streams_of[2], (C,), 0.5, 3.0, jnp.float32)
    kernel_one = noise(streams_of[3], (3, 3, 3, C, C), (27 * C) ** -0.5, 0.078125)
    bias_one = noise(streams_of[4], (C,), 0.5, 3.0, jnp.float32)
    gain_two = jnp.clip(1.0 + 0.1 * jax.random.normal(streams_of[5], (C,), jnp.float32), 0.5, 1.5)
    shift_two = noise(streams_of[6], (C,), 0.5, 3.0, jnp.float32)
    kernel_two = noise(streams_of[7], (3, 3, 3, C, C), (27 * C) ** -0.5, 0.078125)
    bias_two = noise(streams_of[8], (C,), 0.5, 3.0, jnp.float32)
    up_kernel = noise(streams_of[9], (3, 3, C, C2), (9 * C) ** -0.5, 0.15625)
    up_bias = noise(streams_of[10], (C2,), 0.5, 3.0, jnp.float32)
    return {"features": features, "gain_one": gain_one, "shift_one": shift_one, "kernel_one": kernel_one, "bias_one": bias_one, "gain_two": gain_two, "shift_two": shift_two, "kernel_two": kernel_two, "bias_two": bias_two, "up_kernel": up_kernel, "up_bias": up_bias}


epsilon = 1e-06

def group_act(values_in, gain_vec, shift_vec):
    clip_count, frame_count, row_count, col_count, chan_count = values_in.shape
    grouped = values_in.reshape(clip_count, frame_count, row_count, col_count, G, chan_count // G)
    centre_value = lax.optimization_barrier(jnp.mean(grouped, axis=(2, 3, 5), keepdims=True))
    centered = grouped - centre_value
    spread_value = lax.optimization_barrier(jnp.mean(centered * centered, axis=(2, 3, 5), keepdims=True))
    normed = (centered * lax.rsqrt(spread_value + epsilon)).reshape(values_in.shape)
    return jax.nn.silu(normed * gain_vec + shift_vec).astype(jnp.bfloat16)

def causal_taps(padded, kernel, bias_term):
    clip_count, frame_span, row_span, col_count, chan_count = padded.shape
    out_frames = frame_span - 2
    out_rows = row_span - 2
    widened = jnp.pad(padded, ((0, 0), (0, 0), (0, 0), (1, 1), (0, 0)))
    accumulated = jnp.zeros((clip_count * out_frames * out_rows * col_count, kernel.shape[-1]), jnp.float32)
    for time_tap in range(3):
        for row_tap in range(3):
            slab_part = widened[:, time_tap:time_tap + out_frames, row_tap:row_tap + out_rows]
            stacked = jnp.concatenate([slab_part[:, :, :, col_tap:col_tap + col_count] for col_tap in range(3)], axis=-1)
            accumulated = accumulated + jnp.dot(stacked.reshape(-1, 3 * chan_count), kernel[time_tap, row_tap].reshape(3 * chan_count, -1), preferred_element_type=jnp.float32)
    return accumulated.reshape(clip_count, out_frames, out_rows, col_count, -1) + bias_term

def plane_taps(padded, kernel):
    clip_count, frame_count, row_span, col_span, chan_count = padded.shape
    out_rows = row_span - 2
    out_cols = col_span - 2
    accumulated = jnp.zeros((clip_count * frame_count * out_rows * out_cols, kernel.shape[-1]), jnp.float32)
    for row_tap in range(3):
        slab_part = padded[:, :, row_tap:row_tap + out_rows]
        stacked = jnp.concatenate([slab_part[:, :, :, col_tap:col_tap + out_cols] for col_tap in range(3)], axis=-1)
        accumulated = accumulated + jnp.dot(stacked.reshape(-1, 3 * chan_count), kernel[row_tap].reshape(3 * chan_count, -1), preferred_element_type=jnp.float32)
    return accumulated.reshape(clip_count, frame_count, out_rows, out_cols, -1)

def reference(features, gain_one, shift_one, kernel_one, bias_one, gain_two, shift_two, kernel_two, bias_two, up_kernel, up_bias):
    outputs = []
    for clip_index in range(CLIPS):
        source = features[clip_index:clip_index + 1].astype(jnp.float32)
        first_act = group_act(source, gain_one, shift_one)
        first_pad = jnp.pad(first_act, ((0, 0), (2, 0), (1, 1), (0, 0), (0, 0)))
        hidden = causal_taps(first_pad, kernel_one, bias_one).astype(jnp.bfloat16)
        second = group_act(hidden.astype(jnp.float32), gain_two, shift_two)
        second_pad = jnp.pad(second, ((0, 0), (2, 0), (1, 1), (0, 0), (0, 0)))
        joined = (source + causal_taps(second_pad, kernel_two, bias_two)).astype(jnp.bfloat16)
        doubled = jnp.repeat(jnp.repeat(joined, 2, axis=2), 2, axis=3)
        doubled_pad = jnp.pad(doubled, ((0, 0), (0, 0), (1, 1), (1, 1), (0, 0)))
        produced = (plane_taps(doubled_pad, up_kernel) + up_bias).astype(jnp.bfloat16)
        outputs.append(produced.reshape(1, FRAMES, 2 * H, W, 2 * C2))
    return jnp.concatenate(outputs, axis=0)
```

```python
import functools

import jax
import jax.numpy as jnp
from jax import lax
from jax.experimental import pallas as pl
from jax.experimental.pallas import tpu as pltpu
from jax.sharding import PartitionSpec as P

MESH = pl.DeviceIdType.MESH
G = 32
EPS = 1e-06
KP = 640


def split_dot(value, picks):
    m = value.shape[0]
    high = value.astype(jnp.bfloat16).astype(jnp.float32)
    rest = value - high
    mid = rest.astype(jnp.bfloat16).astype(jnp.float32)
    low = rest - mid
    terms = jnp.concatenate([high, mid, low], axis=0).astype(jnp.bfloat16)
    made = jnp.dot(terms, picks, preferred_element_type=jnp.float32)
    return made[0:m] + made[m:2 * m] + made[2 * m:3 * m]


def kernel(
    n,
    feat, g1_h, s1_h, k1, b1_h, g2_h, s2_h, k2, b2_h, uk, ub_h,
    out,
    x_ext, h_ext, j_ext, act1, act2, jact, w1, w2, wup, ukv, vecs, ubv, norm, part, gmap, smap, stats, beside,
    loc_sem, row_send, row_recv, own_send, own_recv, prev_send, prev_recv,
):
    frames, rows, cols, chans = feat.shape
    bf16, f32 = jnp.bfloat16, jnp.float32
    tm = lax.axis_index("tm")
    tile = lax.axis_index("tile")
    up_ok = tile > 0
    down_ok = tile < n - 1
    first = tm == 0
    later = tm > 0
    above = lax.rem(tile + n - 1, n)
    below = lax.rem(tile + 1, n)
    per = chans // G
    half = chans // 2
    inverse = 1.0 / float(n * rows * cols * per)
    old = frames - 2
    pairs = ((old, frames), (0, old))

    def local(i, s, d):
        copy = pltpu.make_async_copy(s, d, loc_sem.at[i])
        copy.start()
        return copy

    load_x = local(0, feat, x_ext.at[:, pl.ds(1, rows)])

    barrier = pltpu.get_barrier_semaphore()
    for d in range(1, n):
        to = lax.rem(tile + d, n)
        pl.semaphore_signal(barrier, inc=1, device_id=(tm, to), device_id_type=MESH)
    pl.semaphore_signal(barrier, inc=1, device_id=(1 - tm, tile), device_id_type=MESH)

    load_u = local(1, uk, ukv)
    load_v = [
        local(4 + i, ref, vecs.at[i])
        for i, ref in enumerate((g1_h, s1_h, b1_h, g2_h, s2_h, b2_h))
    ]
    load_b = local(10, ub_h, ubv)
    load_1 = local(2, k1, w1.at[:, pl.ds(0, 3 * chans)])
    load_2 = local(3, k2, w2.at[:, pl.ds(0, 3 * chans)])

    pending = []

    def send_rows(slot, src, row0, f0, count, dst):
        f = pl.ds(f0, count)

        def remote(i, s, d, who):
            return pltpu.make_async_remote_copy(
                src_ref=s, dst_ref=d,
                send_sem=row_send.at[slot, i], recv_sem=row_recv.at[slot, i],
                device_id=(tm, who), device_id_type=MESH,
            )

        copies = [
            (remote(0, src.at[f, row0 + rows - 1], dst.at[f, 0], below), down_ok, up_ok),
            (remote(1, src.at[f, row0], dst.at[f, rows + 1], above), up_ok, down_ok),
        ]
        for copy, sends, _ in copies:
            pl.when(sends)(copy.start)
        pending.extend(copies)
        return copies

    def wait_rows(copies):
        for copy, _, gets in copies:
            pl.when(gets)(copy.wait_recv)

    sent = []

    def own_copy(slot, d):
        return pltpu.make_async_remote_copy(
            src_ref=stats.at[slot, 0], dst_ref=stats.at[slot, d],
            send_sem=own_send.at[slot], recv_sem=own_recv.at[slot],
            device_id=(tm, lax.rem(tile + d, n)), device_id_type=MESH)

    def own_all(slot):
        view = stats.at[slot, pl.ds(1, n - 1)]
        return pltpu.make_async_remote_copy(
            src_ref=view, dst_ref=view, send_sem=own_send.at[slot], recv_sem=own_recv.at[slot],
            device_id=(tm, below), device_id_type=MESH)

    def send_sums(slot):
        for d in range(1, n):
            own_copy(slot, d).start()
        sent.append(slot)

    def ahead(slot, ref):
        return pltpu.make_async_remote_copy(
            src_ref=ref.at[pl.ds(frames, 2)], dst_ref=ref.at[pl.ds(0, 2)],
            send_sem=prev_send.at[slot], recv_sem=prev_recv.at[slot],
            device_id=(1, tile), device_id_type=MESH)

    def put_sums(slot, flats):
        sums = [jnp.sum(v, axis=0, keepdims=True) for v in flats]
        sums += [jnp.sum(v * v, axis=0, keepdims=True) for v in flats]
        stats[slot, 0, 0:len(sums)] = split_dot(jnp.concatenate(sums, axis=0), gmap[...])

    def norm_from(slot, f0, count, gain):
        total = jnp.sum(stats[slot], axis=0)[0:2 * count]
        both = split_dot(total, smap[...]) * inverse
        mean = both[0:count]
        var = both[count:2 * count] - mean * mean
        scale = 0.5 * (lax.rsqrt(var + EPS) * gain)
        for i in range(count):
            norm[f0 + i, 0:1] = mean[i:i + 1]
            norm[f0 + i, 1:2] = scale[i:i + 1]

    def put_shifted(dst, f, r, value):
        beside[r, 8:8 + cols] = value
        left = beside[r, 7:7 + cols]
        right = beside[r, 9:9 + cols]
        dst[f, r, :, 0:chans] = left.astype(bf16)
        dst[f, r, :, chans:2 * chans] = value.astype(bf16)
        dst[f, r, :, 2 * chans:3 * chans] = right.astype(bf16)

    def act_rows(src, dst, f, which, shift):
        mean, scale = norm[f, 0:1], norm[f, 1:2]
        for r in which:
            scaled = (src[f, r].astype(f32) - mean) * scale + shift
            value = scaled + scaled * jnp.tanh(scaled)
            if r == 0:
                value = jnp.where(up_ok, value, 0.0)
            if r == rows + 1:
                value = jnp.where(down_ok, value, 0.0)
            put_shifted(dst, 2 + f, r, value)

    inner, outer = range(1, rows + 1), (0, rows + 1)

    def conv(act, w, f0, count, taps):
        parts = [
            act[f0 + i:f0 + i + count, j:j + rows].reshape(count * rows * cols, KP)
            for i in taps for j in range(3)
        ]
        return jnp.dot(
            jnp.concatenate(parts, axis=-1),
            w[3 * taps[0]:3 * taps[-1] + 3].reshape(3 * len(taps) * KP, chans),
            preferred_element_type=f32,
        )

    lane = lax.broadcasted_iota(jnp.int32, (chans, 128), 1) * per
    chan = lax.broadcasted_iota(jnp.int32, (chans, 128), 0)
    gmap[...] = jnp.where((chan >= lane) & (chan < lane + per), 1.0, 0.0).astype(bf16)
    lane = lax.broadcasted_iota(jnp.int32, (128, chans), 0) * per
    chan = lax.broadcasted_iota(jnp.int32, (128, chans), 1)
    smap[...] = jnp.where((chan >= lane) & (chan < lane + per), 1.0, 0.0).astype(bf16)
    for slot in (1, 2):
        stats[slot, 0, 4:8] = jnp.zeros((4, 128), f32)

    load_x.wait()
    put_sums(0, [x_ext[f, 1:1 + rows].reshape(rows * cols, chans).astype(f32) for f in range(frames)])
    pl.semaphore_wait(barrier, n)
    send_sums(0)
    rim_x = send_rows(0, feat, 0, 0, frames, x_ext)

    pad = KP - 3 * chans
    beside[:, 0:8] = jnp.zeros((rows + 2, 8, chans), f32)
    beside[:, 8 + cols:16 + cols] = jnp.zeros((rows + 2, 8, chans), f32)
    for act in (act1, act2):
        act[2:2 + frames, :, :, 3 * chans:KP] = jnp.zeros((frames, rows + 2, cols, pad), bf16)
    jact[:, :, :, 3 * chans:KP] = jnp.zeros((frames, rows + 2, cols, pad), bf16)
    w1[:, 3 * chans:KP] = jnp.zeros((9, pad, chans), bf16)
    w2[:, 3 * chans:KP] = jnp.zeros((9, pad, chans), bf16)
    wup[:, :, 3 * chans:KP] = jnp.zeros((2, 2, pad, chans), bf16)

    @pl.when(first)
    def _():
        for act in (act1, act2):
            act[0:2] = jnp.zeros((2, rows + 2, cols, KP), bf16)

    load_u.wait()
    for r in range(2):
        for dy in range(2):
            js = (((0,), (1, 2)) if r == 0 else ((0, 1), (2,)))[dy]
            line = [
                functools.reduce(jnp.add, [ukv[j, k].astype(f32) for j in js]) for k in range(3)
            ]
            zero = jnp.zeros_like(line[0])
            pieces = [(line[0], zero), (line[1] + line[2], line[0] + line[1]), (zero, line[2])]
            for dx, (even, odd) in enumerate(pieces):
                wup[r, dy, dx * chans:(dx + 1) * chans, 0:half] = even.astype(bf16)
                wup[r, dy, dx * chans:(dx + 1) * chans, half:chans] = odd.astype(bf16)
    for copy in load_v:
        copy.wait()
    load_b.wait()
    vecs[6, :, 0:half] = ubv[...]
    vecs[6, :, half:chans] = ubv[...]
    load_1.wait()

    own_all(0).wait_recv()
    norm_from(0, 0, frames, vecs[0])
    shift = 0.5 * vecs[1]
    for f in (2, 3, 0, 1):
        act_rows(x_ext, act1, f, inner, shift)
    wait_rows(rim_x)
    for f in (2, 3):
        act_rows(x_ext, act1, f, outer, shift)

    @pl.when(first)
    def _():
        ahead(0, act1).start()

    for f in (0, 1):
        act_rows(x_ext, act1, f, outer, shift)

    rims = []
    for slot, (f0, f1) in enumerate(pairs):
        if slot == 1:
            @pl.when(later)
            def _():
                ahead(0, act1).wait_recv()

        hidden = (conv(act1, w1, f0, f1 - f0, (0, 1, 2)) + vecs[2]).astype(bf16)
        h_ext[f0:f1, 1:1 + rows] = hidden.reshape(f1 - f0, rows, cols, chans)
        wide = hidden.astype(f32)
        put_sums(1 + slot, [wide[i * rows * cols:(i + 1) * rows * cols] for i in range(f1 - f0)])
        send_sums(1 + slot)
        rims.append(send_rows(1 + slot, h_ext, 1, f0, f1 - f0, h_ext))

    shift = 0.5 * vecs[4]

    def second(slot):
        f0, f1 = pairs[slot]
        own_all(1 + slot).wait_recv()
        norm_from(1 + slot, f0, f1 - f0, vecs[3])
        for f in range(f0, f1):
            act_rows(h_ext, act2, f, inner, shift)
        wait_rows(rims[slot])
        for f in range(f0, f1):
            act_rows(h_ext, act2, f, outer, shift)

    second(0)

    @pl.when(first)
    def _():
        ahead(1, act2).start()

    load_2.wait()
    part[0] = conv(act2, w2, 2, 1, (2,))
    part[1] = conv(act2, w2, 3, 1, (1, 2))
    second(1)

    def joined(slot, made):
        f0, f1 = pairs[slot]
        count = f1 - f0
        base = x_ext[f0:f1, 1:1 + rows].reshape(count * rows * cols, chans).astype(f32)
        value = (base + (made + vecs[5])).astype(bf16)
        j_ext[f0:f1, 1:1 + rows] = value.reshape(count, rows, cols, chans)
        copies = send_rows(3 + slot, j_ext, 1, f0, count, j_ext)
        wide = value.astype(f32).reshape(count, rows, cols, chans)
        for i in range(count):
            for r in range(rows):
                put_shifted(jact, f0 + i, 1 + r, wide[i, r])
        return copies

    made = jnp.concatenate(
        [part[0] + conv(act2, w2, 2, 1, (0, 1)), part[1] + conv(act2, w2, 3, 1, (0,))], axis=0
    )
    rims_j = [joined(0, made)]

    @pl.when(later)
    def _():
        ahead(1, act2).wait_recv()

    rims_j.append(joined(1, conv(act2, w2, 0, 2, (0, 1, 2))))

    bias = vecs[6]

    def up(slot, r, y0, y1):
        f0, f1 = pairs[slot]
        parts = [
            jact[f0:f1, r + dy + y0:r + dy + y1].reshape((f1 - f0) * (y1 - y0) * cols, KP) for dy in range(2)
        ]
        made = jnp.dot(
            jnp.concatenate(parts, axis=-1), wup[r].reshape(2 * KP, chans), preferred_element_type=f32
        ) + bias
        made = made.astype(bf16).reshape(f1 - f0, y1 - y0, cols, chans)
        for i in range(f1 - f0):
            for y in range(y0, y1):
                out[f0 + i, 2 * y + r] = made[i, y - y0]

    for slot in range(2):
        up(slot, 0, 1, rows)
        up(slot, 1, 0, rows - 1)
    for slot in range(2):
        wait_rows(rims_j[slot])
        for f in range(*pairs[slot]):
            put_shifted(jact, f, 0, jnp.where(up_ok, j_ext[f, 0].astype(f32), 0.0))
            put_shifted(jact, f, rows + 1, jnp.where(down_ok, j_ext[f, rows + 1].astype(f32), 0.0))
        up(slot, 0, 0, 1)
        up(slot, 1, rows - 1, rows)

    for copy, sends, _ in pending:
        pl.when(sends)(copy.wait_send)
    for slot in sent:
        own_all(slot).wait_send()

    @pl.when(first)
    def _():
        ahead(0, act1).wait_send()
        ahead(1, act2).wait_send()


def solution(mesh):
    n = mesh.shape["tile"]

    def body(features, g1, s1, k1, b1, g2, s2, k2, b2, uk, ub):
        _, frames, rows, cols, chans = features.shape
        bf16, f32 = jnp.bfloat16, jnp.float32
        hbm = pl.BlockSpec(memory_space=pltpu.HBM)
        vec = lambda v: v.reshape(1, -1)
        dma = pltpu.SemaphoreType.DMA
        made = pl.pallas_call(
            functools.partial(kernel, n),
            out_shape=pltpu.VMEM((frames, 2 * rows, cols, chans), bf16),
            in_specs=[hbm] * 11,
            out_specs=pl.BlockSpec(memory_space=pltpu.VMEM),
            scratch_shapes=[
                pltpu.VMEM((frames, rows + 2, cols, chans), bf16),
                pltpu.VMEM((frames, rows + 2, cols, chans), bf16),
                pltpu.VMEM((frames, rows + 2, cols, chans), bf16),
                pltpu.VMEM((frames + 2, rows + 2, cols, KP), bf16),
                pltpu.VMEM((frames + 2, rows + 2, cols, KP), bf16),
                pltpu.VMEM((frames, rows + 2, cols, KP), bf16),
                pltpu.VMEM((9, KP, chans), bf16),
                pltpu.VMEM((9, KP, chans), bf16),
                pltpu.VMEM((2, 2, KP, chans), bf16),
                pltpu.VMEM(uk.shape, bf16),
                pltpu.VMEM((7, 1, chans), f32),
                pltpu.VMEM((1, chans // 2), f32),
                pltpu.VMEM((frames, 8, chans), f32),
                pltpu.VMEM((2, rows * cols, chans), f32),
                pltpu.VMEM((chans, 128), bf16),
                pltpu.VMEM((128, chans), bf16),
                pltpu.VMEM((3, n, 8, 128), f32),
                pltpu.VMEM((rows + 2, cols + 16, chans), f32),
                dma((11,)),
                dma((5, 2)),
                dma((5, 2)),
                dma((3,)),
                dma((3,)),
                dma((2,)),
                dma((2,)),
            ],
            compiler_params=pltpu.CompilerParams(
                collective_id=0, has_side_effects=True, vmem_limit_bytes=56 * 1024 * 1024
            ),
        )(
            features[0], vec(g1), vec(s1), k1.reshape(9, 3 * chans, chans), vec(b1),
            vec(g2), vec(s2), k2.reshape(9, 3 * chans, chans), vec(b2), uk, vec(ub),
        )
        return made[None]

    return jax.shard_map(
        body,
        mesh=mesh,
        in_specs=(P(None, "tm", "tile", None, None),) + (P(),) * 10,
        out_specs=P(None, "tm", "tile", None, None),
        check_vma=False,
    )
```

```python
import functools

import jax
import jax.numpy as jnp
from jax import lax
from jax.experimental import pallas as pl
from jax.experimental.pallas import tpu as pltpu
from jax.sharding import PartitionSpec as P

MESH = pl.DeviceIdType.MESH
G = 32
EPS = 1e-06
KP = 640


def split_dot(value, picks):
    m = value.shape[0]
    high = value.astype(jnp.bfloat16).astype(jnp.float32)
    rest = value - high
    mid = rest.astype(jnp.bfloat16).astype(jnp.float32)
    low = rest - mid
    terms = jnp.concatenate([high, mid, low], axis=0).astype(jnp.bfloat16)
    made = jnp.dot(terms, picks, preferred_element_type=jnp.float32)
    return made[0:m] + made[m:2 * m] + made[2 * m:3 * m]


def kernel(
    n,
    feat, g1_h, s1_h, k1, b1_h, g2_h, s2_h, k2, b2_h, uk, ub_h,
    out,
    x_own, h_own, act1, act2, jact, w1, w2, wup, ukv, vecs, ubv, norm, sums, gmap, smap, stats, rim_out, rim_in, beside,
    loc_sem, row_send, row_recv, own_send, own_recv, prev_send, prev_recv,
):
    frames, rows, cols, chans = feat.shape
    bf16, f32 = jnp.bfloat16, jnp.float32
    tm = lax.axis_index("tm")
    tile = lax.axis_index("tile")
    up_ok = tile > 0
    down_ok = tile < n - 1
    first = tm == 0
    later = tm > 0
    above = lax.rem(tile + n - 1, n)
    below = lax.rem(tile + 1, n)
    per = chans // G
    half = chans // 2
    inverse = 1.0 / float(n * rows * cols * per)
    old = frames - 2
    pairs = ((old, frames), (0, old))

    def local(i, s, d):
        copy = pltpu.make_async_copy(s, d, loc_sem.at[i])
        copy.start()
        return copy

    load_x = local(0, feat, x_own)

    barrier = pltpu.get_barrier_semaphore()
    for d in range(1, n):
        to = lax.rem(tile + d, n)
        pl.semaphore_signal(barrier, inc=1, device_id=(tm, to), device_id_type=MESH)
    pl.semaphore_signal(barrier, inc=1, device_id=(1 - tm, tile), device_id_type=MESH)

    load_u = local(1, uk, ukv)
    load_v = [
        local(4 + i, ref, vecs.at[i])
        for i, ref in enumerate((g1_h, s1_h, b1_h, g2_h, s2_h, b2_h))
    ]
    load_b = local(10, ub_h, ubv)
    load_1 = local(2, k1, w1.at[:, pl.ds(0, 3 * chans)])
    load_2 = local(3, k2, w2.at[:, pl.ds(0, 3 * chans)])

    alone = pl.when(tile >= 0)

    pending = []

    def pack(k, d, f, row):
        low = cols // 2
        side = chans - 128
        rim_out[k, d, f, 0:cols] = row[:, 0:128]
        rim_out[k, d, f, cols:cols + low, 0:side] = row[0:low, 128:chans]
        rim_out[k, d, f, cols:cols + low, 64:64 + side] = row[low:cols, 128:chans]

    def unpack(k, d, f):
        low = cols // 2
        side = chans - 128
        edge = rim_in[k, d, f].astype(f32)
        rest = jnp.concatenate([edge[cols:cols + low, 0:side], edge[cols:cols + low, 64:64 + side]], axis=0)
        return jnp.concatenate([edge[0:cols], rest], axis=-1)

    def send_rows(k, slot, f0, f1):
        f = pl.ds(f0, f1 - f0)

        def remote(d, who):
            return pltpu.make_async_remote_copy(
                src_ref=rim_out.at[k, d, f], dst_ref=rim_in.at[k, d, f],
                send_sem=row_send.at[slot, d], recv_sem=row_recv.at[slot, d],
                device_id=(tm, who), device_id_type=MESH,
            )

        copies = [(remote(0, below), down_ok, up_ok), (remote(1, above), up_ok, down_ok)]
        for copy, sends, _ in copies:
            pl.when(sends)(copy.start)
        pending.extend(copies)
        return copies

    def wait_rows(copies):
        for copy, _, gets in copies:
            pl.when(gets)(copy.wait_recv)

    sent = []

    def own_copy(slot, d):
        return pltpu.make_async_remote_copy(
            src_ref=stats.at[slot, 0, pl.ds(0, 2)], dst_ref=stats.at[slot, d, pl.ds(0, 2)],
            send_sem=own_send.at[slot], recv_sem=own_recv.at[slot],
            device_id=(tm, lax.rem(tile + d, n)), device_id_type=MESH)

    def own_all(slot):
        view = stats.at[slot, pl.ds(1, n - 1), pl.ds(0, 2)]
        return pltpu.make_async_remote_copy(
            src_ref=view, dst_ref=view, send_sem=own_send.at[slot], recv_sem=own_recv.at[slot],
            device_id=(tm, below), device_id_type=MESH)

    def send_sums(slot):
        for d in range(1, n):
            own_copy(slot, d).start()
        sent.append(slot)

    def ahead(k, part, ref):
        lines = (pl.ds(1, rows), 0, rows + 1)[part]
        return pltpu.make_async_remote_copy(
            src_ref=ref.at[pl.ds(frames, 2), lines], dst_ref=ref.at[pl.ds(0, 2), lines],
            send_sem=prev_send.at[k, part], recv_sem=prev_recv.at[k, part],
            device_id=(1, tile), device_id_type=MESH)

    def give(k, parts, ref):
        @pl.when(first)
        def _():
            for part in parts:
                ahead(k, part, ref).start()

    def take(k, parts, ref):
        @pl.when(later)
        def _():
            for part in parts:
                ahead(k, part, ref).wait_recv()

    block_of = lax.broadcasted_iota(jnp.int32, (frames, 128), 1) // G
    block = jnp.where(block_of == lax.broadcasted_iota(jnp.int32, (frames, 128), 0), 1.0, 0.0)

    def put_sums(slot):
        @alone
        def _():
            made = split_dot(sums[...], gmap[...])
            for i in range(2):
                stats[slot, 0, i:i + 1] = jnp.sum(made[i * frames:(i + 1) * frames] * block, axis=0, keepdims=True)

    def add_sums(f, value, fresh):
        for i, v in enumerate((value, value * value)):
            line = slice(i * frames + f, i * frames + f + 1)
            total = jnp.sum(v, axis=0, keepdims=True)
            sums[line] = total if fresh else sums[line] + total

    def norm_from(slot, gain):
        @alone
        def _():
            total = jnp.sum(stats[slot, :, 0:2], axis=0)
            spread = jnp.concatenate([total[0:1] * block, total[1:2] * block], axis=0)
            both = split_dot(spread, smap[...]) * inverse
            mean = both[0:frames]
            var = both[frames:2 * frames] - mean * mean
            norm[0:frames] = mean
            norm[8:8 + frames] = 0.5 * (lax.rsqrt(var + EPS) * gain)

    def put_shifted(dst, f, r, value):
        beside[r, 8:8 + cols] = value
        left = beside[r, 7:7 + cols]
        right = beside[r, 9:9 + cols]
        dst[f, r, :, 0:chans] = left.astype(bf16)
        dst[f, r, :, chans:2 * chans] = value.astype(bf16)
        dst[f, r, :, 2 * chans:3 * chans] = right.astype(bf16)

    def act_row(dst, f, r, value, shift, ok=None):
        scaled = (value - norm[f:f + 1]) * norm[8 + f:9 + f] + shift
        made = scaled + scaled * jnp.tanh(scaled)
        if ok is not None:
            made = jnp.where(ok, made, 0.0)
        put_shifted(dst, 2 + f, r, made)

    def act_inner(src, dst, f, shift):
        for r in range(rows):
            act_row(dst, f, 1 + r, src[f, r].astype(f32), shift)

    def act_outer(k, dst, f, shift):
        act_row(dst, f, 0, unpack(k, 0, f), shift, up_ok)
        act_row(dst, f, rows + 1, unpack(k, 1, f), shift, down_ok)

    inner, outer = tuple(range(1, rows - 1)), (0, rows - 1)

    def lines_of(ref, f0, f1, which, j):
        if which == inner:
            return ref[f0:f1, 1 + j:rows - 1 + j]
        return jnp.concatenate([ref[f0:f1, y + j:y + j + 1] for y in which], axis=1)

    def conv(act, w, pair, which):
        f0, f1 = pair
        m = (f1 - f0) * len(which) * cols
        parts = [
            lines_of(act, f0 + i, f1 + i, which, j).reshape(m, KP) for i in range(3) for j in range(3)
        ]
        return jnp.dot(
            jnp.concatenate(parts, axis=-1), w[...].reshape(9 * KP, chans), preferred_element_type=f32
        )

    lane = lax.broadcasted_iota(jnp.int32, (chans, 128), 1) % G
    chan = lax.broadcasted_iota(jnp.int32, (chans, 128), 0) // per
    gmap[...] = jnp.where(lane == chan, 1.0, 0.0).astype(bf16)
    lane = lax.broadcasted_iota(jnp.int32, (128, chans), 0) % G
    chan = lax.broadcasted_iota(jnp.int32, (128, chans), 1) // per
    smap[...] = jnp.where(lane == chan, 1.0, 0.0).astype(bf16)

    load_x.wait()
    for f in range(frames):
        add_sums(f, x_own[f].reshape(rows * cols, chans).astype(f32), True)
    put_sums(0)
    for f in range(frames):
        pack(0, 0, f, x_own[f, rows - 1])
        pack(0, 1, f, x_own[f, 0])
    pl.semaphore_wait(barrier, n)
    send_sums(0)
    rim_x = send_rows(0, 0, 0, frames)

    pad = KP - 3 * chans
    beside[:, 0:8] = jnp.zeros((rows + 2, 8, chans), f32)
    beside[:, 8 + cols:16 + cols] = jnp.zeros((rows + 2, 8, chans), f32)
    for act in (act1, act2):
        act[2:2 + frames, :, :, 3 * chans:KP] = jnp.zeros((frames, rows + 2, cols, pad), bf16)
    jact[:, :, :, 3 * chans:KP] = jnp.zeros((frames, rows + 2, cols, pad), bf16)
    w1[:, 3 * chans:KP] = jnp.zeros((9, pad, chans), bf16)
    w2[:, 3 * chans:KP] = jnp.zeros((9, pad, chans), bf16)
    wup[:, :, 3 * chans:KP] = jnp.zeros((2, 2, pad, chans), bf16)

    @pl.when(first)
    def _():
        for act in (act1, act2):
            act[0:2] = jnp.zeros((2, rows + 2, cols, KP), bf16)

    load_u.wait()
    for r in range(2):
        for dy in range(2):
            js = (((0,), (1, 2)) if r == 0 else ((0, 1), (2,)))[dy]
            line = [
                functools.reduce(jnp.add, [ukv[j, k].astype(f32) for j in js]) for k in range(3)
            ]
            zero = jnp.zeros_like(line[0])
            pieces = [(line[0], zero), (line[1] + line[2], line[0] + line[1]), (zero, line[2])]
            for dx, (even, odd) in enumerate(pieces):
                wup[r, dy, dx * chans:(dx + 1) * chans, 0:half] = even.astype(bf16)
                wup[r, dy, dx * chans:(dx + 1) * chans, half:chans] = odd.astype(bf16)
    for copy in load_v:
        copy.wait()
    load_b.wait()
    vecs[6, :, 0:half] = ubv[...]
    vecs[6, :, half:chans] = ubv[...]
    load_1.wait()
    load_2.wait()

    def stage(k, src, act, gain, shift, rims, piece, after):
        own_all(k).wait_recv()
        norm_from(k, gain)
        for f in range(*pairs[0]):
            act_inner(src, act, f, shift)
        give(k, (0,), act)
        for f in range(*pairs[1]):
            act_inner(src, act, f, shift)
        alone(functools.partial(piece, pairs[0], inner))
        take(k, (0,), act)
        alone(functools.partial(piece, pairs[1], inner))
        for copies in rims:
            wait_rows(copies)
        for f in range(*pairs[0]):
            act_outer(k, act, f, shift)
        give(k, (1, 2), act)
        for f in range(*pairs[1]):
            act_outer(k, act, f, shift)
        alone(functools.partial(piece, pairs[0], outer))
        after(0)
        take(k, (1, 2), act)
        alone(functools.partial(piece, pairs[1], outer))
        after(1)

    def each(pair, which):
        at = 0
        for f in range(*pair):
            for y in which:
                yield f, y, slice(at * cols, (at + 1) * cols)
                at += 1

    def hidden_piece(pair, which):
        made = (conv(act1, w1, pair, which) + vecs[2]).astype(bf16)
        wide = made.astype(f32)
        m = len(which) * cols
        for f in range(*pair):
            add_sums(f, wide[(f - pair[0]) * m:(f - pair[0] + 1) * m], which == inner)
        for f, y, at in each(pair, which):
            h_own[f, y] = made[at]
            if y == rows - 1:
                pack(1, 0, f, made[at])
            if y == 0:
                pack(1, 1, f, made[at])

    rim_h, rim_j = [], []

    def hidden_after(slot):
        if slot == 1:
            put_sums(1)
            send_sums(1)
        rim_h.append(send_rows(1, 1 + slot, *pairs[slot]))

    def joined_piece(pair, which):
        base = lines_of(x_own, pair[0], pair[1], which, 0) if which == outer else x_own[pair[0]:pair[1], 1:rows - 1]
        base = base.reshape(-1, chans).astype(f32)
        made = (base + (conv(act2, w2, pair, which) + vecs[5])).astype(bf16)
        wide = made.astype(f32)
        for f, y, at in each(pair, which):
            if y == rows - 1:
                pack(2, 0, f, made[at])
            if y == 0:
                pack(2, 1, f, made[at])
            put_shifted(jact, f, 1 + y, wide[at])

    def joined_after(slot):
        rim_j.append(send_rows(2, 3 + slot, *pairs[slot]))

    stage(0, x_own, act1, vecs[0], 0.5 * vecs[1], [rim_x], hidden_piece, hidden_after)
    stage(1, h_own, act2, vecs[3], 0.5 * vecs[4], rim_h, joined_piece, joined_after)

    def up(pair, r, y0, y1):
        f0, f1 = pair
        parts = [
            jact[f0:f1, r + dy + y0:r + dy + y1].reshape((f1 - f0) * (y1 - y0) * cols, KP) for dy in range(2)
        ]
        made = jnp.dot(
            jnp.concatenate(parts, axis=-1), wup[r].reshape(2 * KP, chans), preferred_element_type=f32
        ) + vecs[6]
        made = made.astype(bf16).reshape(f1 - f0, y1 - y0, cols, chans)
        for i in range(f1 - f0):
            for y in range(y0, y1):
                out[f0 + i, 2 * y + r] = made[i, y - y0]

    @alone
    def _():
        up((0, frames), 0, 1, rows)

    @alone
    def _():
        up((0, frames), 1, 0, rows - 1)

    for slot in range(2):
        wait_rows(rim_j[slot])
        for f in range(*pairs[slot]):
            put_shifted(jact, f, 0, jnp.where(up_ok, unpack(2, 0, f), 0.0))
            put_shifted(jact, f, rows + 1, jnp.where(down_ok, unpack(2, 1, f), 0.0))

        @alone
        def _():
            up(pairs[slot], 0, 0, 1)
            up(pairs[slot], 1, rows - 1, rows)

    for copy, sends, _ in pending:
        pl.when(sends)(copy.wait_send)
    for slot in sent:
        own_all(slot).wait_send()

    @pl.when(first)
    def _():
        for k, act in enumerate((act1, act2)):
            for part in range(3):
                ahead(k, part, act).wait_send()


def solution(mesh):
    n = mesh.shape["tile"]

    def body(features, g1, s1, k1, b1, g2, s2, k2, b2, uk, ub):
        _, frames, rows, cols, chans = features.shape
        bf16, f32 = jnp.bfloat16, jnp.float32
        hbm = pl.BlockSpec(memory_space=pltpu.HBM)
        vec = lambda v: v.reshape(1, -1)
        dma = pltpu.SemaphoreType.DMA
        made = pl.pallas_call(
            functools.partial(kernel, n),
            out_shape=pltpu.VMEM((frames, 2 * rows, cols, chans), bf16),
            in_specs=[hbm] * 11,
            out_specs=pl.BlockSpec(memory_space=pltpu.VMEM),
            scratch_shapes=[
                pltpu.VMEM((frames, rows, cols, chans), bf16),
                pltpu.VMEM((frames, rows, cols, chans), bf16),
                pltpu.VMEM((frames + 2, rows + 2, cols, KP), bf16),
                pltpu.VMEM((frames + 2, rows + 2, cols, KP), bf16),
                pltpu.VMEM((frames, rows + 2, cols, KP), bf16),
                pltpu.VMEM((9, KP, chans), bf16),
                pltpu.VMEM((9, KP, chans), bf16),
                pltpu.VMEM((2, 2, KP, chans), bf16),
                pltpu.VMEM(uk.shape, bf16),
                pltpu.VMEM((7, 1, chans), f32),
                pltpu.VMEM((1, chans // 2), f32),
                pltpu.VMEM((16, chans), f32),
                pltpu.VMEM((2 * frames, chans), f32),
                pltpu.VMEM((chans, 128), bf16),
                pltpu.VMEM((128, chans), bf16),
                pltpu.VMEM((2, n, 8, 128), f32),
                pltpu.VMEM((3, 2, frames, cols + cols // 2, 128), bf16),
                pltpu.VMEM((3, 2, frames, cols + cols // 2, 128), bf16),
                pltpu.VMEM((rows + 2, cols + 16, chans), f32),
                dma((11,)),
                dma((5, 2)),
                dma((5, 2)),
                dma((2,)),
                dma((2,)),
                dma((2, 3)),
                dma((2, 3)),
            ],
            compiler_params=pltpu.CompilerParams(
                collective_id=0, has_side_effects=True, vmem_limit_bytes=56 * 1024 * 1024
            ),
        )(
            features[0], vec(g1), vec(s1), k1.reshape(9, 3 * chans, chans), vec(b1),
            vec(g2), vec(s2), k2.reshape(9, 3 * chans, chans), vec(b2), uk, vec(ub),
        )
        return made[None]

    return jax.shard_map(
        body,
        mesh=mesh,
        in_specs=(P(None, "tm", "tile", None, None),) + (P(),) * 10,
        out_specs=P(None, "tm", "tile", None, None),
        check_vma=False,
    )
```

```python
import functools

import jax
import jax.numpy as jnp
from jax import lax
from jax.experimental import pallas as pl
from jax.experimental.pallas import tpu as pltpu
from jax.sharding import PartitionSpec as P

MESH = pl.DeviceIdType.MESH
G = 32
EPS = 1e-06
KP = 640


def split_dot(value, picks):
    m = value.shape[0]
    high = value.astype(jnp.bfloat16).astype(jnp.float32)
    rest = value - high
    mid = rest.astype(jnp.bfloat16).astype(jnp.float32)
    low = rest - mid
    terms = jnp.concatenate([high, mid, low], axis=0).astype(jnp.bfloat16)
    made = jnp.dot(terms, picks, preferred_element_type=jnp.float32)
    return made[0:m] + made[m:2 * m] + made[2 * m:3 * m]


def kernel(
    n,
    feat, g1_h, s1_h, k1, b1_h, g2_h, s2_h, k2, b2_h, uk, ub_h,
    out,
    x_own, h_own, act1, act2, jact, w1, w2, wup, ukv, vecs, ubv, norm, sums, gmap, smap, stats, rim_out, rim_in, beside,
    loc_sem, row_send, row_recv, own_send, own_recv, prev_send, prev_recv,
):
    frames, rows, cols, chans = feat.shape
    bf16, f32 = jnp.bfloat16, jnp.float32
    tm = lax.axis_index("tm")
    tile = lax.axis_index("tile")
    up_ok = tile > 0
    down_ok = tile < n - 1
    first = tm == 0
    later = tm > 0
    above = lax.rem(tile + n - 1, n)
    below = lax.rem(tile + 1, n)
    per = chans // G
    half = chans // 2
    inverse = 1.0 / float(n * rows * cols * per)
    old = frames - 2
    pairs = ((old, frames), (0, old))

    def local(i, s, d):
        copy = pltpu.make_async_copy(s, d, loc_sem.at[i])
        copy.start()
        return copy

    load_x = local(0, feat, x_own)

    barrier = pltpu.get_barrier_semaphore()
    for d in range(1, n):
        to = lax.rem(tile + d, n)
        pl.semaphore_signal(barrier, inc=1, device_id=(tm, to), device_id_type=MESH)
    pl.semaphore_signal(barrier, inc=1, device_id=(1 - tm, tile), device_id_type=MESH)

    load_u = local(1, uk, ukv)
    load_v = [
        local(4 + i, ref, vecs.at[i])
        for i, ref in enumerate((g1_h, s1_h, b1_h, g2_h, s2_h, b2_h))
    ]
    load_b = local(10, ub_h, ubv)
    load_1 = local(2, k1, w1.at[:, pl.ds(0, 3 * chans)])
    load_2 = local(3, k2, w2.at[:, pl.ds(0, 3 * chans)])

    alone = pl.when(tile >= 0)

    pending = []

    def pack(k, d, f, row):
        low = cols // 2
        side = chans - 128
        rim_out[k, d, f, 0:cols] = row[:, 0:128]
        rim_out[k, d, f, cols:cols + low, 0:side] = row[0:low, 128:chans]
        rim_out[k, d, f, cols:cols + low, 64:64 + side] = row[low:cols, 128:chans]

    def unpack(k, d, f):
        low = cols // 2
        side = chans - 128
        edge = rim_in[k, d, f].astype(f32)
        rest = jnp.concatenate([edge[cols:cols + low, 0:side], edge[cols:cols + low, 64:64 + side]], axis=0)
        return jnp.concatenate([edge[0:cols], rest], axis=-1)

    def send_rows(k, slot, f0, f1):
        f = pl.ds(f0, f1 - f0)

        def remote(d, who):
            return pltpu.make_async_remote_copy(
                src_ref=rim_out.at[k, d, f], dst_ref=rim_in.at[k, d, f],
                send_sem=row_send.at[slot, d], recv_sem=row_recv.at[slot, d],
                device_id=(tm, who), device_id_type=MESH,
            )

        copies = [(remote(0, below), down_ok, up_ok), (remote(1, above), up_ok, down_ok)]
        for copy, sends, _ in copies:
            pl.when(sends)(copy.start)
        pending.extend(copies)
        return copies

    def wait_rows(copies):
        for copy, _, gets in copies:
            pl.when(gets)(copy.wait_recv)

    sent = []

    def own_copy(slot, d):
        return pltpu.make_async_remote_copy(
            src_ref=stats.at[slot, 0, pl.ds(0, 2)], dst_ref=stats.at[slot, d, pl.ds(0, 2)],
            send_sem=own_send.at[slot], recv_sem=own_recv.at[slot],
            device_id=(tm, lax.rem(tile + d, n)), device_id_type=MESH)

    def own_all(slot):
        view = stats.at[slot, pl.ds(1, n - 1), pl.ds(0, 2)]
        return pltpu.make_async_remote_copy(
            src_ref=view, dst_ref=view, send_sem=own_send.at[slot], recv_sem=own_recv.at[slot],
            device_id=(tm, below), device_id_type=MESH)

    def send_sums(slot):
        for d in range(1, n):
            own_copy(slot, d).start()
        sent.append(slot)

    def ahead(k, part, ref):
        lines = (pl.ds(1, rows), 0, rows + 1)[part]
        return pltpu.make_async_remote_copy(
            src_ref=ref.at[pl.ds(frames, 2), lines], dst_ref=ref.at[pl.ds(0, 2), lines],
            send_sem=prev_send.at[k, part], recv_sem=prev_recv.at[k, part],
            device_id=(1, tile), device_id_type=MESH)

    def give(k, parts, ref):
        @pl.when(first)
        def _():
            for part in parts:
                ahead(k, part, ref).start()

    def take(k, parts, ref):
        @pl.when(later)
        def _():
            for part in parts:
                ahead(k, part, ref).wait_recv()

    block_of = lax.broadcasted_iota(jnp.int32, (frames, 128), 1) // G
    block = jnp.where(block_of == lax.broadcasted_iota(jnp.int32, (frames, 128), 0), 1.0, 0.0)

    def put_sums(slot):
        @alone
        def _():
            made = split_dot(sums[...], gmap[...])
            for i in range(2):
                stats[slot, 0, i:i + 1] = jnp.sum(made[i * frames:(i + 1) * frames] * block, axis=0, keepdims=True)

    def add_sums(f, value, fresh):
        for i, v in enumerate((value, value * value)):
            line = slice(i * frames + f, i * frames + f + 1)
            total = jnp.sum(v, axis=0, keepdims=True)
            sums[line] = total if fresh else sums[line] + total

    def norm_from(slot, gain):
        @alone
        def _():
            total = jnp.sum(stats[slot, :, 0:2], axis=0)
            spread = jnp.concatenate([total[0:1] * block, total[1:2] * block], axis=0)
            both = split_dot(spread, smap[...]) * inverse
            mean = both[0:frames]
            var = both[frames:2 * frames] - mean * mean
            norm[0:frames] = mean
            norm[8:8 + frames] = 0.5 * (lax.rsqrt(var + EPS) * gain)

    def put_shifted(dst, f, r, value):
        beside[r, 8:8 + cols] = value
        left = beside[r, 7:7 + cols]
        right = beside[r, 9:9 + cols]
        dst[f, r, :, 0:chans] = left.astype(bf16)
        dst[f, r, :, chans:2 * chans] = value.astype(bf16)
        dst[f, r, :, 2 * chans:3 * chans] = right.astype(bf16)

    def act_row(dst, f, r, value, shift, ok=None):
        scaled = (value - norm[f:f + 1]) * norm[8 + f:9 + f] + shift
        made = scaled + scaled * jnp.tanh(scaled)
        if ok is not None:
            made = jnp.where(ok, made, 0.0)
        put_shifted(dst, 2 + f, r, made)

    def act_inner(src, dst, f, shift):
        for r in range(rows):
            act_row(dst, f, 1 + r, src[f, r].astype(f32), shift)

    def act_outer(k, dst, f, shift):
        act_row(dst, f, 0, unpack(k, 0, f), shift, up_ok)
        act_row(dst, f, rows + 1, unpack(k, 1, f), shift, down_ok)

    inner, outer = tuple(range(1, rows - 1)), (0, rows - 1)

    def lines_of(ref, f0, f1, which, j):
        if which == inner:
            return ref[f0:f1, 1 + j:rows - 1 + j]
        return jnp.concatenate([ref[f0:f1, y + j:y + j + 1] for y in which], axis=1)

    def conv(act, w, pair, which):
        f0, f1 = pair
        m = (f1 - f0) * len(which) * cols
        parts = [
            lines_of(act, f0 + i, f1 + i, which, j).reshape(m, KP) for i in range(3) for j in range(3)
        ]
        return jnp.dot(
            jnp.concatenate(parts, axis=-1), w[...].reshape(9 * KP, chans), preferred_element_type=f32
        )

    lane = lax.broadcasted_iota(jnp.int32, (chans, 128), 1) % G
    chan = lax.broadcasted_iota(jnp.int32, (chans, 128), 0) // per
    gmap[...] = jnp.where(lane == chan, 1.0, 0.0).astype(bf16)
    lane = lax.broadcasted_iota(jnp.int32, (128, chans), 0) % G
    chan = lax.broadcasted_iota(jnp.int32, (128, chans), 1) // per
    smap[...] = jnp.where(lane == chan, 1.0, 0.0).astype(bf16)

    load_x.wait()
    for f in range(frames):
        add_sums(f, x_own[f].reshape(rows * cols, chans).astype(f32), True)
    put_sums(0)
    for f in range(frames):
        pack(0, 0, f, x_own[f, rows - 1])
        pack(0, 1, f, x_own[f, 0])
    pl.semaphore_wait(barrier, n)
    send_sums(0)
    rim_x = send_rows(0, 0, 0, frames)

    pad = KP - 3 * chans
    beside[:, 0:8] = jnp.zeros((rows + 2, 8, chans), f32)
    beside[:, 8 + cols:16 + cols] = jnp.zeros((rows + 2, 8, chans), f32)
    for act in (act1, act2):
        act[2:2 + frames, :, :, 3 * chans:KP] = jnp.zeros((frames, rows + 2, cols, pad), bf16)
    jact[:, :, :, 3 * chans:KP] = jnp.zeros((frames, rows + 2, cols, pad), bf16)
    w1[:, 3 * chans:KP] = jnp.zeros((9, pad, chans), bf16)
    w2[:, 3 * chans:KP] = jnp.zeros((9, pad, chans), bf16)
    wup[:, :, 3 * chans:KP] = jnp.zeros((2, 2, pad, chans), bf16)

    @pl.when(first)
    def _():
        for act in (act1, act2):
            act[0:2] = jnp.zeros((2, rows + 2, cols, KP), bf16)

    load_u.wait()
    for r in range(2):
        for dy in range(2):
            js = (((0,), (1, 2)) if r == 0 else ((0, 1), (2,)))[dy]
            line = [
                functools.reduce(jnp.add, [ukv[j, k].astype(f32) for j in js]) for k in range(3)
            ]
            zero = jnp.zeros_like(line[0])
            pieces = [(line[0], zero), (line[1] + line[2], line[0] + line[1]), (zero, line[2])]
            for dx, (even, odd) in enumerate(pieces):
                wup[r, dy, dx * chans:(dx + 1) * chans, 0:half] = even.astype(bf16)
                wup[r, dy, dx * chans:(dx + 1) * chans, half:chans] = odd.astype(bf16)
    for copy in load_v:
        copy.wait()
    load_b.wait()
    vecs[6, :, 0:half] = ubv[...]
    vecs[6, :, half:chans] = ubv[...]
    load_1.wait()
    load_2.wait()

    def stage(k, src, act, gain, shift, rims, piece, after):
        def outer_rows(pair):
            for f in range(*pair):
                act_outer(k, act, f, shift)

        own_all(k).wait_recv()
        norm_from(k, gain)
        for f in range(*pairs[0]):
            act_inner(src, act, f, shift)
        give(k, (0,), act)
        if k == 1:
            for copies in rims:
                wait_rows(copies)
            outer_rows(pairs[0])
            give(k, (1, 2), act)
        for f in range(*pairs[1]):
            act_inner(src, act, f, shift)

        @alone
        def _():
            piece(pairs[0], inner)
            if k == 1:
                outer_rows(pairs[1])

        if k == 0:
            for copies in rims:
                wait_rows(copies)
            outer_rows(pairs[0])
            give(k, (1, 2), act)
            outer_rows(pairs[1])
        alone(functools.partial(piece, pairs[0], outer))
        after(0)
        if k == 0:
            take(k, (0,), act)
            alone(functools.partial(piece, pairs[1], inner))
            take(k, (1, 2), act)
            alone(functools.partial(piece, pairs[1], outer))
            after(1)
        else:
            take(k, (0, 1, 2), act)
            alone(functools.partial(piece, pairs[1], outer))
            after(1)
            alone(functools.partial(piece, pairs[1], inner))

    def each(pair, which):
        at = 0
        for f in range(*pair):
            for y in which:
                yield f, y, slice(at * cols, (at + 1) * cols)
                at += 1

    def hidden_piece(pair, which):
        made = (conv(act1, w1, pair, which) + vecs[2]).astype(bf16)
        wide = made.astype(f32)
        m = len(which) * cols
        for f in range(*pair):
            add_sums(f, wide[(f - pair[0]) * m:(f - pair[0] + 1) * m], which == inner)
        for f, y, at in each(pair, which):
            h_own[f, y] = made[at]
            if y == rows - 1:
                pack(1, 0, f, made[at])
            if y == 0:
                pack(1, 1, f, made[at])

    rim_h, rim_j = [], []

    def hidden_after(slot):
        if slot == 1:
            put_sums(1)
            send_sums(1)
        rim_h.append(send_rows(1, 1 + slot, *pairs[slot]))

    def joined_piece(pair, which):
        base = lines_of(x_own, pair[0], pair[1], which, 0) if which == outer else x_own[pair[0]:pair[1], 1:rows - 1]
        base = base.reshape(-1, chans).astype(f32)
        made = (base + (conv(act2, w2, pair, which) + vecs[5])).astype(bf16)
        wide = made.astype(f32)
        for f, y, at in each(pair, which):
            if y == rows - 1:
                pack(2, 0, f, made[at])
            if y == 0:
                pack(2, 1, f, made[at])
            put_shifted(jact, f, 1 + y, wide[at])

    def joined_after(slot):
        rim_j.append(send_rows(2, 3 + slot, *pairs[slot]))

    stage(0, x_own, act1, vecs[0], 0.5 * vecs[1], [rim_x], hidden_piece, hidden_after)
    stage(1, h_own, act2, vecs[3], 0.5 * vecs[4], rim_h, joined_piece, joined_after)

    def up(pair, r, y0, y1):
        f0, f1 = pair
        parts = [
            jact[f0:f1, r + dy + y0:r + dy + y1].reshape((f1 - f0) * (y1 - y0) * cols, KP) for dy in range(2)
        ]
        made = jnp.dot(
            jnp.concatenate(parts, axis=-1), wup[r].reshape(2 * KP, chans), preferred_element_type=f32
        ) + vecs[6]
        made = made.astype(bf16).reshape(f1 - f0, y1 - y0, cols, chans)
        for i in range(f1 - f0):
            for y in range(y0, y1):
                out[f0 + i, 2 * y + r] = made[i, y - y0]

    @alone
    def _():
        up((0, frames), 0, 1, rows)

    @alone
    def _():
        up((0, frames), 1, 0, rows - 1)

    for slot in range(2):
        wait_rows(rim_j[slot])
        for f in range(*pairs[slot]):
            put_shifted(jact, f, 0, jnp.where(up_ok, unpack(2, 0, f), 0.0))
            put_shifted(jact, f, rows + 1, jnp.where(down_ok, unpack(2, 1, f), 0.0))

        @alone
        def _():
            up(pairs[slot], 0, 0, 1)
            up(pairs[slot], 1, rows - 1, rows)

    for copy, sends, _ in pending:
        pl.when(sends)(copy.wait_send)
    for slot in sent:
        own_all(slot).wait_send()

    @pl.when(first)
    def _():
        for k, act in enumerate((act1, act2)):
            for part in range(3):
                ahead(k, part, act).wait_send()


def solution(mesh):
    n = mesh.shape["tile"]

    def body(features, g1, s1, k1, b1, g2, s2, k2, b2, uk, ub):
        _, frames, rows, cols, chans = features.shape
        bf16, f32 = jnp.bfloat16, jnp.float32
        hbm = pl.BlockSpec(memory_space=pltpu.HBM)
        vec = lambda v: v.reshape(1, -1)
        dma = pltpu.SemaphoreType.DMA
        made = pl.pallas_call(
            functools.partial(kernel, n),
            out_shape=pltpu.VMEM((frames, 2 * rows, cols, chans), bf16),
            in_specs=[hbm] * 11,
            out_specs=pl.BlockSpec(memory_space=pltpu.VMEM),
            scratch_shapes=[
                pltpu.VMEM((frames, rows, cols, chans), bf16),
                pltpu.VMEM((frames, rows, cols, chans), bf16),
                pltpu.VMEM((frames + 2, rows + 2, cols, KP), bf16),
                pltpu.VMEM((frames + 2, rows + 2, cols, KP), bf16),
                pltpu.VMEM((frames, rows + 2, cols, KP), bf16),
                pltpu.VMEM((9, KP, chans), bf16),
                pltpu.VMEM((9, KP, chans), bf16),
                pltpu.VMEM((2, 2, KP, chans), bf16),
                pltpu.VMEM(uk.shape, bf16),
                pltpu.VMEM((7, 1, chans), f32),
                pltpu.VMEM((1, chans // 2), f32),
                pltpu.VMEM((16, chans), f32),
                pltpu.VMEM((2 * frames, chans), f32),
                pltpu.VMEM((chans, 128), bf16),
                pltpu.VMEM((128, chans), bf16),
                pltpu.VMEM((2, n, 8, 128), f32),
                pltpu.VMEM((3, 2, frames, cols + cols // 2, 128), bf16),
                pltpu.VMEM((3, 2, frames, cols + cols // 2, 128), bf16),
                pltpu.VMEM((rows + 2, cols + 16, chans), f32),
                dma((11,)),
                dma((5, 2)),
                dma((5, 2)),
                dma((2,)),
                dma((2,)),
                dma((2, 3)),
                dma((2, 3)),
            ],
            compiler_params=pltpu.CompilerParams(
                collective_id=0, has_side_effects=True, vmem_limit_bytes=56 * 1024 * 1024
            ),
        )(
            features[0], vec(g1), vec(s1), k1.reshape(9, 3 * chans, chans), vec(b1),
            vec(g2), vec(s2), k2.reshape(9, 3 * chans, chans), vec(b2), uk, vec(ub),
        )
        return made[None]

    return jax.shard_map(
        body,
        mesh=mesh,
        in_specs=(P(None, "tm", "tile", None, None),) + (P(),) * 10,
        out_specs=P(None, "tm", "tile", None, None),
        check_vma=False,
    )
```

```python
import functools

import jax
import jax.numpy as jnp
from jax import lax
from jax.experimental import pallas as pl
from jax.experimental.pallas import tpu as pltpu
from jax.sharding import PartitionSpec as P

MESH = pl.DeviceIdType.MESH
G = 32
EPS = 1e-06
KP = 640


def split_dot(value, picks):
    m = value.shape[0]
    high = value.astype(jnp.bfloat16).astype(jnp.float32)
    rest = value - high
    mid = rest.astype(jnp.bfloat16).astype(jnp.float32)
    low = rest - mid
    terms = jnp.concatenate([high, mid, low], axis=0).astype(jnp.bfloat16)
    made = jnp.dot(terms, picks, preferred_element_type=jnp.float32)
    return made[0:m] + made[m:2 * m] + made[2 * m:3 * m]


def kernel(
    n,
    feat, g1_h, s1_h, k1, b1_h, g2_h, s2_h, k2, b2_h, uk, ub_h,
    out,
    x_own, h_own, act1, act2, jact, w1, w2, wup, ukv, vecs, ubv, norm, norm_out, norm_in, sums, gmap, smap, stats, rim_out, rim_in, rim_prev, beside,
    loc_sem, row_send, row_recv, own_send, own_recv, prev_send, prev_recv,
):
    frames, rows, cols, chans = feat.shape
    bf16, f32 = jnp.bfloat16, jnp.float32
    tm = lax.axis_index("tm")
    tile = lax.axis_index("tile")
    up_ok = tile > 0
    down_ok = tile < n - 1
    first = tm == 0
    later = tm > 0
    above = lax.rem(tile + n - 1, n)
    below = lax.rem(tile + 1, n)
    per = chans // G
    half = chans // 2
    inverse = 1.0 / float(n * rows * cols * per)
    old = frames - 2
    pairs = ((old, frames), (0, old))

    def local(i, s, d):
        copy = pltpu.make_async_copy(s, d, loc_sem.at[i])
        copy.start()
        return copy

    load_x = local(0, feat, x_own.at[pl.ds(2, frames)])

    barrier = pltpu.get_barrier_semaphore()
    for d in range(1, n):
        to = lax.rem(tile + d, n)
        pl.semaphore_signal(barrier, inc=1, device_id=(tm, to), device_id_type=MESH)
    pl.semaphore_signal(barrier, inc=1, device_id=(1 - tm, tile), device_id_type=MESH)

    load_u = local(1, uk, ukv)
    load_v = [
        local(4 + i, ref, vecs.at[i])
        for i, ref in enumerate((g1_h, s1_h, b1_h, g2_h, s2_h, b2_h))
    ]
    load_b = local(10, ub_h, ubv)
    load_1 = local(2, k1, w1.at[:, pl.ds(0, 3 * chans)])
    load_2 = local(3, k2, w2.at[:, pl.ds(0, 3 * chans)])

    alone = pl.when(tile >= 0)

    pending = []

    def pack(k, d, f, row):
        low = cols // 2
        side = chans - 128
        rim_out[k, d, f, 0:cols] = row[:, 0:128]
        rim_out[k, d, f, cols:cols + low, 0:side] = row[0:low, 128:chans]
        rim_out[k, d, f, cols:cols + low, 64:64 + side] = row[low:cols, 128:chans]

    def unpack(edge):
        low = cols // 2
        side = chans - 128
        edge = edge.astype(f32)
        rest = jnp.concatenate([edge[cols:cols + low, 0:side], edge[cols:cols + low, 64:64 + side]], axis=0)
        return jnp.concatenate([edge[0:cols], rest], axis=-1)

    def send_rows(k, slot, f0, f1):
        f = pl.ds(f0, f1 - f0)

        def remote(d, who):
            return pltpu.make_async_remote_copy(
                src_ref=rim_out.at[k, d, f], dst_ref=rim_in.at[k, d, f],
                send_sem=row_send.at[slot, d], recv_sem=row_recv.at[slot, d],
                device_id=(tm, who), device_id_type=MESH,
            )

        copies = [(remote(0, below), down_ok, up_ok), (remote(1, above), up_ok, down_ok)]
        for copy, sends, _ in copies:
            pl.when(sends)(copy.start)
        pending.extend(copies)
        return copies

    def wait_rows(copies):
        for copy, _, gets in copies:
            pl.when(gets)(copy.wait_recv)

    sent = []

    def own_copy(slot, d):
        return pltpu.make_async_remote_copy(
            src_ref=stats.at[slot, 0, pl.ds(0, 2)], dst_ref=stats.at[slot, d, pl.ds(0, 2)],
            send_sem=own_send.at[slot], recv_sem=own_recv.at[slot],
            device_id=(tm, lax.rem(tile + d, n)), device_id_type=MESH)

    def own_all(slot):
        view = stats.at[slot, pl.ds(1, n - 1), pl.ds(0, 2)]
        return pltpu.make_async_remote_copy(
            src_ref=view, dst_ref=view, send_sem=own_send.at[slot], recv_sem=own_recv.at[slot],
            device_id=(tm, below), device_id_type=MESH)

    def send_sums(slot):
        for d in range(1, n):
            own_copy(slot, d).start()
        sent.append(slot)

    def ahead(k, part):
        held = feat.at[pl.ds(old, 2)] if k == 0 else h_own.at[pl.ds(frames, 2)]
        source, target = (
            (held, (x_own, h_own)[k].at[pl.ds(0, 2)]),
            (norm_out.at[k], norm_in.at[k]),
            (rim_in.at[k, pl.ds(0, 2), pl.ds(old, 2)], rim_prev.at[k]),
        )[part]
        return pltpu.make_async_remote_copy(
            src_ref=source, dst_ref=target,
            send_sem=prev_send.at[k, part], recv_sem=prev_recv.at[k, part],
            device_id=(1, tile), device_id_type=MESH)

    def give(k, part):
        @pl.when(first)
        def _():
            ahead(k, part).start()

    block_of = lax.broadcasted_iota(jnp.int32, (frames, 128), 1) // G
    block = jnp.where(block_of == lax.broadcasted_iota(jnp.int32, (frames, 128), 0), 1.0, 0.0)

    def put_sums(slot):
        @alone
        def _():
            made = split_dot(sums[...], gmap[...])
            for i in range(2):
                stats[slot, 0, i:i + 1] = jnp.sum(made[i * frames:(i + 1) * frames] * block, axis=0, keepdims=True)

    def add_sums(f, value, fresh):
        for i, v in enumerate((value, value * value)):
            line = slice(i * frames + f, i * frames + f + 1)
            total = jnp.sum(v, axis=0, keepdims=True)
            sums[line] = total if fresh else sums[line] + total

    def norm_from(slot, gain):
        @alone
        def _():
            total = jnp.sum(stats[slot, :, 0:2], axis=0)
            spread = jnp.concatenate([total[0:1] * block, total[1:2] * block], axis=0)
            both = split_dot(spread, smap[...]) * inverse
            mean = both[0:frames]
            var = both[frames:2 * frames] - mean * mean
            scale = 0.5 * (lax.rsqrt(var + EPS) * gain)
            norm[0:frames] = mean
            norm[8:8 + frames] = scale
            norm_out[slot, 0:2] = mean[old:frames]
            norm_out[slot, 2:4] = scale[old:frames]

    def put_shifted(dst, f, r, value):
        beside[r, 8:8 + cols] = value
        left = beside[r, 7:7 + cols]
        right = beside[r, 9:9 + cols]
        dst[f, r, :, 0:chans] = left.astype(bf16)
        dst[f, r, :, chans:2 * chans] = value.astype(bf16)
        dst[f, r, :, 2 * chans:3 * chans] = right.astype(bf16)

    def act_row(dst, f, r, value, mean, scale, shift, ok=None):
        scaled = (value - mean) * scale + shift
        made = scaled + scaled * jnp.tanh(scaled)
        if ok is not None:
            made = jnp.where(ok, made, 0.0)
        put_shifted(dst, f, r, made)

    def act_inner(src, dst, f, mean, scale, shift):
        for r in range(rows):
            act_row(dst, f, 1 + r, src[f, r].astype(f32), mean, scale, shift)

    def act_outer(top, bottom, dst, f, mean, scale, shift):
        act_row(dst, f, 0, unpack(top), mean, scale, shift, up_ok)
        act_row(dst, f, rows + 1, unpack(bottom), mean, scale, shift, down_ok)

    inner, outer = tuple(range(1, rows - 1)), (0, rows - 1)

    def lines_of(ref, f0, f1, which, j):
        if which == inner:
            return ref[f0:f1, 1 + j:rows - 1 + j]
        return jnp.concatenate([ref[f0:f1, y + j:y + j + 1] for y in which], axis=1)

    def conv(act, w, pair, which):
        f0, f1 = pair
        m = (f1 - f0) * len(which) * cols
        parts = [
            lines_of(act, f0 + i, f1 + i, which, j).reshape(m, KP) for i in range(3) for j in range(3)
        ]
        return jnp.dot(
            jnp.concatenate(parts, axis=-1), w[...].reshape(9 * KP, chans), preferred_element_type=f32
        )

    lane = lax.broadcasted_iota(jnp.int32, (chans, 128), 1) % G
    chan = lax.broadcasted_iota(jnp.int32, (chans, 128), 0) // per
    gmap[...] = jnp.where(lane == chan, 1.0, 0.0).astype(bf16)
    lane = lax.broadcasted_iota(jnp.int32, (128, chans), 0) % G
    chan = lax.broadcasted_iota(jnp.int32, (128, chans), 1) // per
    smap[...] = jnp.where(lane == chan, 1.0, 0.0).astype(bf16)

    load_x.wait()
    for f in range(frames):
        add_sums(f, x_own[2 + f].reshape(rows * cols, chans).astype(f32), True)
    put_sums(0)
    for f in range(frames):
        pack(0, 0, f, x_own[2 + f, rows - 1])
        pack(0, 1, f, x_own[2 + f, 0])
    pl.semaphore_wait(barrier, n)
    send_sums(0)
    rim_x = send_rows(0, 0, 0, frames)
    give(0, 0)

    pad = KP - 3 * chans
    beside[:, 0:8] = jnp.zeros((rows + 2, 8, chans), f32)
    beside[:, 8 + cols:16 + cols] = jnp.zeros((rows + 2, 8, chans), f32)
    for act in (act1, act2):
        act[2:2 + frames, :, :, 3 * chans:KP] = jnp.zeros((frames, rows + 2, cols, pad), bf16)
    jact[:, :, :, 3 * chans:KP] = jnp.zeros((frames, rows + 2, cols, pad), bf16)
    w1[:, 3 * chans:KP] = jnp.zeros((9, pad, chans), bf16)
    w2[:, 3 * chans:KP] = jnp.zeros((9, pad, chans), bf16)
    wup[:, :, 3 * chans:KP] = jnp.zeros((2, 2, pad, chans), bf16)

    @pl.when(first)
    def _():
        for act in (act1, act2):
            act[0:2] = jnp.zeros((2, rows + 2, cols, KP), bf16)

    load_u.wait()
    for r in range(2):
        for dy in range(2):
            js = (((0,), (1, 2)) if r == 0 else ((0, 1), (2,)))[dy]
            line = [
                functools.reduce(jnp.add, [ukv[j, k].astype(f32) for j in js]) for k in range(3)
            ]
            zero = jnp.zeros_like(line[0])
            pieces = [(line[0], zero), (line[1] + line[2], line[0] + line[1]), (zero, line[2])]
            for dx, (even, odd) in enumerate(pieces):
                wup[r, dy, dx * chans:(dx + 1) * chans, 0:half] = even.astype(bf16)
                wup[r, dy, dx * chans:(dx + 1) * chans, half:chans] = odd.astype(bf16)
    for copy in load_v:
        copy.wait()
    load_b.wait()
    vecs[6, :, 0:half] = ubv[...]
    vecs[6, :, half:chans] = ubv[...]
    load_1.wait()
    load_2.wait()

    def stage(k, src, act, gain, shift, rims, piece, after):
        def inner_rows():
            for f in range(frames):
                act_inner(src, act, 2 + f, norm[f:f + 1], norm[8 + f:9 + f], shift)

        def outer_rows():
            for copies in rims:
                wait_rows(copies)
            give(k, 2)
            for f in range(frames):
                act_outer(rim_in[k, 0, f], rim_in[k, 1, f], act, 2 + f, norm[f:f + 1], norm[8 + f:9 + f], shift)

        own_all(k).wait_recv()
        norm_from(k, gain)
        give(k, 1)
        inner_rows()
        if k == 0:
            alone(functools.partial(piece, pairs[0], inner))
        outer_rows()
        alone(functools.partial(piece, pairs[0], outer))
        after(0)

        @pl.when(later)
        def _():
            for part in range(3):
                ahead(k, part).wait_recv()
            for f in range(2):
                mean, scale = norm_in[k, f:f + 1], norm_in[k, 2 + f:3 + f]
                act_inner(src, act, f, mean, scale, shift)
                act_outer(rim_prev[k, 0, f], rim_prev[k, 1, f], act, f, mean, scale, shift)

        alone(functools.partial(piece, pairs[1], outer))
        after(1)
        if k == 1:
            alone(functools.partial(piece, pairs[0], inner))
        alone(functools.partial(piece, pairs[1], inner))

    def each(pair, which):
        at = 0
        for f in range(*pair):
            for y in which:
                yield f, y, slice(at * cols, (at + 1) * cols)
                at += 1

    def hidden_piece(pair, which):
        made = (conv(act1, w1, pair, which) + vecs[2]).astype(bf16)
        wide = made.astype(f32)
        m = len(which) * cols
        for f in range(*pair):
            add_sums(f, wide[(f - pair[0]) * m:(f - pair[0] + 1) * m], (which == inner) == (pair == pairs[0]))
        for f, y, at in each(pair, which):
            h_own[2 + f, y] = made[at]
            if y == rows - 1:
                pack(1, 0, f, made[at])
            if y == 0:
                pack(1, 1, f, made[at])

    rim_h, rim_j = [], []

    def hidden_after(slot):
        rim_h.append(send_rows(1, 1 + slot, *pairs[slot]))
        if slot == 0:
            give(1, 0)

    def joined_piece(pair, which):
        f0, f1 = 2 + pair[0], 2 + pair[1]
        base = lines_of(x_own, f0, f1, which, 0) if which == outer else x_own[f0:f1, 1:rows - 1]
        base = base.reshape(-1, chans).astype(f32)
        made = (base + (conv(act2, w2, pair, which) + vecs[5])).astype(bf16)
        wide = made.astype(f32)
        for f, y, at in each(pair, which):
            if y == rows - 1:
                pack(2, 0, f, made[at])
            if y == 0:
                pack(2, 1, f, made[at])
            put_shifted(jact, f, 1 + y, wide[at])

    def joined_after(slot):
        rim_j.append(send_rows(2, 3 + slot, *pairs[slot]))

    stage(0, x_own, act1, vecs[0], 0.5 * vecs[1], [rim_x], hidden_piece, hidden_after)
    put_sums(1)
    send_sums(1)
    stage(1, h_own, act2, vecs[3], 0.5 * vecs[4], rim_h, joined_piece, joined_after)

    def up(pair, r, y0, y1):
        f0, f1 = pair
        parts = [
            jact[f0:f1, r + dy + y0:r + dy + y1].reshape((f1 - f0) * (y1 - y0) * cols, KP) for dy in range(2)
        ]
        made = jnp.dot(
            jnp.concatenate(parts, axis=-1), wup[r].reshape(2 * KP, chans), preferred_element_type=f32
        ) + vecs[6]
        made = made.astype(bf16).reshape(f1 - f0, y1 - y0, cols, chans)
        for i in range(f1 - f0):
            for y in range(y0, y1):
                out[f0 + i, 2 * y + r] = made[i, y - y0]

    @alone
    def _():
        up((0, frames), 0, 1, rows)

    @alone
    def _():
        up((0, frames), 1, 0, rows - 1)

    for slot in range(2):
        wait_rows(rim_j[slot])
        for f in range(*pairs[slot]):
            put_shifted(jact, f, 0, jnp.where(up_ok, unpack(rim_in[2, 0, f]), 0.0))
            put_shifted(jact, f, rows + 1, jnp.where(down_ok, unpack(rim_in[2, 1, f]), 0.0))

        @alone
        def _():
            up(pairs[slot], 0, 0, 1)
            up(pairs[slot], 1, rows - 1, rows)

    for copy, sends, _ in pending:
        pl.when(sends)(copy.wait_send)
    for slot in sent:
        own_all(slot).wait_send()

    @pl.when(first)
    def _():
        for k in range(2):
            for part in range(3):
                ahead(k, part).wait_send()


def solution(mesh):
    n = mesh.shape["tile"]

    def body(features, g1, s1, k1, b1, g2, s2, k2, b2, uk, ub):
        _, frames, rows, cols, chans = features.shape
        bf16, f32 = jnp.bfloat16, jnp.float32
        hbm = pl.BlockSpec(memory_space=pltpu.HBM)
        vec = lambda v: v.reshape(1, -1)
        dma = pltpu.SemaphoreType.DMA
        made = pl.pallas_call(
            functools.partial(kernel, n),
            out_shape=pltpu.VMEM((frames, 2 * rows, cols, chans), bf16),
            in_specs=[hbm] * 11,
            out_specs=pl.BlockSpec(memory_space=pltpu.VMEM),
            scratch_shapes=[
                pltpu.VMEM((frames + 2, rows, cols, chans), bf16),
                pltpu.VMEM((frames + 2, rows, cols, chans), bf16),
                pltpu.VMEM((frames + 2, rows + 2, cols, KP), bf16),
                pltpu.VMEM((frames + 2, rows + 2, cols, KP), bf16),
                pltpu.VMEM((frames, rows + 2, cols, KP), bf16),
                pltpu.VMEM((9, KP, chans), bf16),
                pltpu.VMEM((9, KP, chans), bf16),
                pltpu.VMEM((2, 2, KP, chans), bf16),
                pltpu.VMEM(uk.shape, bf16),
                pltpu.VMEM((7, 1, chans), f32),
                pltpu.VMEM((1, chans // 2), f32),
                pltpu.VMEM((16, chans), f32),
                pltpu.VMEM((2, 4, chans), f32),
                pltpu.VMEM((2, 4, chans), f32),
                pltpu.VMEM((2 * frames, chans), f32),
                pltpu.VMEM((chans, 128), bf16),
                pltpu.VMEM((128, chans), bf16),
                pltpu.VMEM((2, n, 8, 128), f32),
                pltpu.VMEM((3, 2, frames, cols + cols // 2, 128), bf16),
                pltpu.VMEM((3, 2, frames, cols + cols // 2, 128), bf16),
                pltpu.VMEM((2, 2, 2, cols + cols // 2, 128), bf16),
                pltpu.VMEM((rows + 2, cols + 16, chans), f32),
                dma((11,)),
                dma((5, 2)),
                dma((5, 2)),
                dma((2,)),
                dma((2,)),
                dma((2, 3)),
                dma((2, 3)),
            ],
            compiler_params=pltpu.CompilerParams(
                collective_id=0, has_side_effects=True, vmem_limit_bytes=56 * 1024 * 1024
            ),
        )(
            features[0], vec(g1), vec(s1), k1.reshape(9, 3 * chans, chans), vec(b1),
            vec(g2), vec(s2), k2.reshape(9, 3 * chans, chans), vec(b2), uk, vec(ub),
        )
        return made[None]

    return jax.shard_map(
        body,
        mesh=mesh,
        in_specs=(P(None, "tm", "tile", None, None),) + (P(),) * 10,
        out_specs=P(None, "tm", "tile", None, None),
        check_vma=False,
    )
```

```python
import functools

import jax
import jax.numpy as jnp
from jax import lax
from jax.experimental import pallas as pl
from jax.experimental.pallas import tpu as pltpu
from jax.sharding import PartitionSpec as P

MESH = pl.DeviceIdType.MESH
G = 32
EPS = 1e-06
KP = 640


def split_dot(value, picks):
    m = value.shape[0]
    high = value.astype(jnp.bfloat16).astype(jnp.float32)
    rest = value - high
    mid = rest.astype(jnp.bfloat16).astype(jnp.float32)
    low = rest - mid
    terms = jnp.concatenate([high, mid, low], axis=0).astype(jnp.bfloat16)
    made = jnp.dot(terms, picks, preferred_element_type=jnp.float32)
    return made[0:m] + made[m:2 * m] + made[2 * m:3 * m]


def kernel(
    n,
    feat, g1_h, s1_h, k1, b1_h, g2_h, s2_h, k2, b2_h, uk, ub_h,
    out,
    x_own, h_own, act1, act2, jact, w1, w2, wup, ukv, vecs, ubv, norm, norm_out, norm_in, sums, gmap, smap, stats, rim_out, rim_in, rim_prev, beside,
    loc_sem, row_send, row_recv, own_send, own_recv, prev_send, prev_recv,
):
    frames, rows, cols, chans = feat.shape
    bf16, f32 = jnp.bfloat16, jnp.float32
    tm = lax.axis_index("tm")
    tile = lax.axis_index("tile")
    up_ok = tile > 0
    down_ok = tile < n - 1
    first = tm == 0
    later = tm > 0
    above = lax.rem(tile + n - 1, n)
    below = lax.rem(tile + 1, n)
    per = chans // G
    half = chans // 2
    inverse = 1.0 / float(n * rows * cols * per)
    old = frames - 2
    pairs = ((old, frames), (0, old))

    def local(i, s, d):
        copy = pltpu.make_async_copy(s, d, loc_sem.at[i])
        copy.start()
        return copy

    load_x = local(0, feat, x_own.at[pl.ds(2, frames)])

    far = sorted(range(1, n), key=lambda d: -min(d, n - d))

    barrier = pltpu.get_barrier_semaphore()
    for d in far:
        to = lax.rem(tile + d, n)
        pl.semaphore_signal(barrier, inc=1, device_id=(tm, to), device_id_type=MESH)
    pl.semaphore_signal(barrier, inc=1, device_id=(1 - tm, tile), device_id_type=MESH)

    load_u = local(1, uk, ukv)
    load_v = [
        local(4 + i, ref, vecs.at[i])
        for i, ref in enumerate((g1_h, s1_h, b1_h, g2_h, s2_h, b2_h))
    ]
    load_b = local(10, ub_h, ubv)
    load_1 = local(2, k1, w1.at[:, pl.ds(0, 3 * chans)])
    load_2 = local(3, k2, w2.at[:, pl.ds(0, 3 * chans)])

    alone = pl.when(tile >= 0)

    pending = []

    def pack(k, d, f, row):
        low = cols // 2
        side = chans - 128
        rim_out[k, d, f, 0:cols] = row[:, 0:128]
        rim_out[k, d, f, cols:cols + low, 0:side] = row[0:low, 128:chans]
        rim_out[k, d, f, cols:cols + low, 64:64 + side] = row[low:cols, 128:chans]

    def unpack(edge):
        low = cols // 2
        side = chans - 128
        edge = edge.astype(f32)
        rest = jnp.concatenate([edge[cols:cols + low, 0:side], edge[cols:cols + low, 64:64 + side]], axis=0)
        return jnp.concatenate([edge[0:cols], rest], axis=-1)

    def send_rows(k, slot, f0, f1):
        f = pl.ds(f0, f1 - f0)

        def remote(d, who):
            return pltpu.make_async_remote_copy(
                src_ref=rim_out.at[k, d, f], dst_ref=rim_in.at[k, d, f],
                send_sem=row_send.at[slot, d], recv_sem=row_recv.at[slot, d],
                device_id=(tm, who), device_id_type=MESH,
            )

        copies = [(remote(0, below), down_ok, up_ok), (remote(1, above), up_ok, down_ok)]
        for copy, sends, _ in copies:
            pl.when(sends)(copy.start)
        pending.extend(copies)
        return copies

    def wait_rows(copies):
        for copy, _, gets in copies:
            pl.when(gets)(copy.wait_recv)

    sent = []

    def own_copy(slot, d):
        return pltpu.make_async_remote_copy(
            src_ref=stats.at[slot, 0, pl.ds(0, 2)], dst_ref=stats.at[slot, d, pl.ds(0, 2)],
            send_sem=own_send.at[slot], recv_sem=own_recv.at[slot],
            device_id=(tm, lax.rem(tile + d, n)), device_id_type=MESH)

    def own_all(slot):
        view = stats.at[slot, pl.ds(1, n - 1), pl.ds(0, 2)]
        return pltpu.make_async_remote_copy(
            src_ref=view, dst_ref=view, send_sem=own_send.at[slot], recv_sem=own_recv.at[slot],
            device_id=(tm, below), device_id_type=MESH)

    def send_sums(slot):
        for d in range(1, n):
            own_copy(slot, d).start()
        sent.append(slot)

    def ahead(k, part):
        held = feat.at[pl.ds(old, 2)] if k == 0 else h_own.at[pl.ds(frames, 2)]
        source, target = (
            (held, (x_own, h_own)[k].at[pl.ds(0, 2)]),
            (norm_out.at[k], norm_in.at[k]),
            (rim_in.at[k, pl.ds(0, 2), pl.ds(old, 2)], rim_prev.at[k]),
        )[part]
        return pltpu.make_async_remote_copy(
            src_ref=source, dst_ref=target,
            send_sem=prev_send.at[k, part], recv_sem=prev_recv.at[k, part],
            device_id=(1, tile), device_id_type=MESH)

    def give(k, part):
        @pl.when(first)
        def _():
            ahead(k, part).start()

    block_of = lax.broadcasted_iota(jnp.int32, (frames, 128), 1) // G
    block = jnp.where(block_of == lax.broadcasted_iota(jnp.int32, (frames, 128), 0), 1.0, 0.0)

    def put_sums(slot, f0, f1):
        @alone
        def _():
            made = split_dot(sums[...], gmap[...])
            for i in range(2):
                picked = made[i * frames + f0:i * frames + f1] * block[f0:f1]
                stats[slot, 0, i:i + 1] = jnp.sum(picked, axis=0, keepdims=True)

    def add_sums(f, value, fresh):
        for i, v in enumerate((value, value * value)):
            line = slice(i * frames + f, i * frames + f + 1)
            total = jnp.sum(v, axis=0, keepdims=True)
            sums[line] = total if fresh else sums[line] + total

    def norm_from(k, slot, f0, f1, gain):
        @alone
        def _():
            total = jnp.sum(stats[slot, :, 0:2], axis=0)
            spread = jnp.concatenate([total[0:1] * block, total[1:2] * block], axis=0)
            both = split_dot(spread, smap[...]) * inverse
            mean = both[0:frames]
            var = both[frames:2 * frames] - mean * mean
            scale = 0.5 * (lax.rsqrt(var + EPS) * gain)
            norm[f0:f1] = mean[f0:f1]
            norm[8 + f0:8 + f1] = scale[f0:f1]
            if f1 == frames:
                norm_out[k, 0:2] = mean[old:frames]
                norm_out[k, 2:4] = scale[old:frames]

    def put_shifted(dst, f, r, value):
        at = lax.broadcasted_iota(jnp.int32, (cols, 1), 0)
        left = jnp.where(at == 0, 0.0, pltpu.roll(value, 1, 0))
        right = jnp.where(at == cols - 1, 0.0, pltpu.roll(value, cols - 1, 0))
        dst[f, r, :, 0:chans] = left.astype(bf16)
        dst[f, r, :, chans:2 * chans] = value.astype(bf16)
        dst[f, r, :, 2 * chans:3 * chans] = right.astype(bf16)

    def act_row(dst, f, r, value, mean, scale, shift, ok=None):
        scaled = (value - mean) * scale + shift
        made = scaled + scaled * jnp.tanh(scaled)
        if ok is not None:
            made = jnp.where(ok, made, 0.0)
        put_shifted(dst, f, r, made)

    def act_inner(src, dst, f, mean, scale, shift):
        for r in range(rows):
            act_row(dst, f, 1 + r, src[f, r].astype(f32), mean, scale, shift)

    def act_outer(top, bottom, dst, f, mean, scale, shift):
        act_row(dst, f, 0, unpack(top), mean, scale, shift, up_ok)
        act_row(dst, f, rows + 1, unpack(bottom), mean, scale, shift, down_ok)

    inner, outer = tuple(range(1, rows - 1)), (0, rows - 1)

    def lines_of(ref, f0, f1, which, j):
        if which == inner:
            return ref[f0:f1, 1 + j:rows - 1 + j]
        return jnp.concatenate([ref[f0:f1, y + j:y + j + 1] for y in which], axis=1)

    def conv(act, w, pair, which):
        f0, f1 = pair
        m = (f1 - f0) * len(which) * cols
        parts = [
            lines_of(act, f0 + i, f1 + i, which, j).reshape(m, KP) for i in range(3) for j in range(3)
        ]
        return jnp.dot(
            jnp.concatenate(parts, axis=-1), w[...].reshape(9 * KP, chans), preferred_element_type=f32
        )

    lane = lax.broadcasted_iota(jnp.int32, (chans, 128), 1) % G
    chan = lax.broadcasted_iota(jnp.int32, (chans, 128), 0) // per
    gmap[...] = jnp.where(lane == chan, 1.0, 0.0).astype(bf16)
    lane = lax.broadcasted_iota(jnp.int32, (128, chans), 0) % G
    chan = lax.broadcasted_iota(jnp.int32, (128, chans), 1) // per
    smap[...] = jnp.where(lane == chan, 1.0, 0.0).astype(bf16)

    load_x.wait()
    for f in range(frames):
        add_sums(f, x_own[2 + f].reshape(rows * cols, chans).astype(f32), True)
    put_sums(0, 0, frames)
    for f in range(frames):
        pack(0, 0, f, x_own[2 + f, rows - 1])
        pack(0, 1, f, x_own[2 + f, 0])
    pl.semaphore_wait(barrier, n)
    send_sums(0)
    rim_x = send_rows(0, 0, 0, frames)
    give(0, 0)

    pad = KP - 3 * chans
    beside[:, 0:8] = jnp.zeros((rows + 2, 8, chans), f32)
    beside[:, 8 + cols:16 + cols] = jnp.zeros((rows + 2, 8, chans), f32)
    for act in (act1, act2):
        act[2:2 + frames, :, :, 3 * chans:KP] = jnp.zeros((frames, rows + 2, cols, pad), bf16)
    jact[:, :, :, 3 * chans:KP] = jnp.zeros((frames, rows + 2, cols, pad), bf16)
    w1[:, 3 * chans:KP] = jnp.zeros((9, pad, chans), bf16)
    w2[:, 3 * chans:KP] = jnp.zeros((9, pad, chans), bf16)
    wup[:, :, 3 * chans:KP] = jnp.zeros((2, 2, pad, chans), bf16)

    @pl.when(first)
    def _():
        for act in (act1, act2):
            act[0:2] = jnp.zeros((2, rows + 2, cols, KP), bf16)

    load_u.wait()
    for r in range(2):
        for dy in range(2):
            js = (((0,), (1, 2)) if r == 0 else ((0, 1), (2,)))[dy]
            line = [
                functools.reduce(jnp.add, [ukv[j, k].astype(f32) for j in js]) for k in range(3)
            ]
            zero = jnp.zeros_like(line[0])
            pieces = [(line[0], zero), (line[1] + line[2], line[0] + line[1]), (zero, line[2])]
            for dx, (even, odd) in enumerate(pieces):
                wup[r, dy, dx * chans:(dx + 1) * chans, 0:half] = even.astype(bf16)
                wup[r, dy, dx * chans:(dx + 1) * chans, half:chans] = odd.astype(bf16)
    for copy in load_v:
        copy.wait()
    load_b.wait()
    vecs[6, :, 0:half] = ubv[...]
    vecs[6, :, half:chans] = ubv[...]
    load_1.wait()
    load_2.wait()

    def stage(k, src, act, gain, shift, rims, piece, after):
        def own(f):
            return norm[f:f + 1], norm[8 + f:9 + f], shift

        def inner_rows(f0, f1):
            for f in range(f0, f1):
                act_inner(src, act, 2 + f, *own(f))

        def outer_rows(f0, f1):
            for f in range(f0, f1):
                act_outer(rim_in[k, 0, f], rim_in[k, 1, f], act, 2 + f, *own(f))

        def take_rims(copies):
            for copy in copies:
                wait_rows(copy)
            give(k, 2)

        if k == 0:
            own_all(0).wait_recv()
            norm_from(0, 0, 0, frames, gain)
            give(0, 1)
            inner_rows(0, frames)
            alone(functools.partial(piece, pairs[0], inner))
            take_rims(rims)
            outer_rows(0, frames)
        else:
            take_rims(rims[0:1])
            own_all(1).wait_recv()
            norm_from(1, 1, *pairs[0], gain)
            give(1, 1)
            inner_rows(*pairs[0])
            outer_rows(*pairs[0])
            wait_rows(rims[1])
            own_all(2).wait_recv()
            norm_from(1, 2, *pairs[1], gain)
            inner_rows(*pairs[1])
            outer_rows(*pairs[1])
        alone(functools.partial(piece, pairs[0], outer))
        after(0)

        @pl.when(later)
        def _():
            for part in range(3):
                ahead(k, part).wait_recv()
            for f in range(2):
                mean, scale = norm_in[k, f:f + 1], norm_in[k, 2 + f:3 + f]
                act_inner(src, act, f, mean, scale, shift)
                act_outer(rim_prev[k, 0, f], rim_prev[k, 1, f], act, f, mean, scale, shift)

        alone(functools.partial(piece, pairs[1], outer))
        after(1)
        if k == 1:
            alone(functools.partial(piece, pairs[0], inner))
        alone(functools.partial(piece, pairs[1], inner))

    def each(pair, which):
        at = 0
        for f in range(*pair):
            for y in which:
                yield f, y, slice(at * cols, (at + 1) * cols)
                at += 1

    def hidden_piece(pair, which):
        made = (conv(act1, w1, pair, which) + vecs[2]).astype(bf16)
        wide = made.astype(f32)
        m = len(which) * cols
        for f in range(*pair):
            add_sums(f, wide[(f - pair[0]) * m:(f - pair[0] + 1) * m], (which == inner) == (pair == pairs[0]))
        for f, y, at in each(pair, which):
            h_own[2 + f, y] = made[at]
            if y == rows - 1:
                pack(1, 0, f, made[at])
            if y == 0:
                pack(1, 1, f, made[at])

    rim_h, rim_j = [], []

    def hidden_after(slot):
        rim_h.append(send_rows(1, 1 + slot, *pairs[slot]))
        if slot == 0:
            give(1, 0)
            put_sums(1, *pairs[0])
            send_sums(1)

    def joined_piece(pair, which):
        f0, f1 = 2 + pair[0], 2 + pair[1]
        base = lines_of(x_own, f0, f1, which, 0) if which == outer else x_own[f0:f1, 1:rows - 1]
        base = base.reshape(-1, chans).astype(f32)
        made = (base + (conv(act2, w2, pair, which) + vecs[5])).astype(bf16)
        wide = made.astype(f32)
        for f, y, at in each(pair, which):
            if y == rows - 1:
                pack(2, 0, f, made[at])
            if y == 0:
                pack(2, 1, f, made[at])
            put_shifted(jact, f, 1 + y, wide[at])

    def joined_after(slot):
        rim_j.append(send_rows(2, 3 + slot, *pairs[slot]))

    stage(0, x_own, act1, vecs[0], 0.5 * vecs[1], [rim_x], hidden_piece, hidden_after)
    put_sums(2, *pairs[1])
    send_sums(2)
    stage(1, h_own, act2, vecs[3], 0.5 * vecs[4], rim_h, joined_piece, joined_after)

    def up(pair, r, y0, y1):
        f0, f1 = pair
        parts = [
            jact[f0:f1, r + dy + y0:r + dy + y1].reshape((f1 - f0) * (y1 - y0) * cols, KP) for dy in range(2)
        ]
        made = jnp.dot(
            jnp.concatenate(parts, axis=-1), wup[r].reshape(2 * KP, chans), preferred_element_type=f32
        ) + vecs[6]
        made = made.astype(bf16).reshape(f1 - f0, y1 - y0, cols, chans)
        for i in range(f1 - f0):
            for y in range(y0, y1):
                out[f0 + i, 2 * y + r] = made[i, y - y0]

    @alone
    def _():
        up((0, frames), 0, 1, rows)

    @alone
    def _():
        up((0, frames), 1, 0, rows - 1)

    for slot in range(2):
        wait_rows(rim_j[slot])
        for f in range(*pairs[slot]):
            put_shifted(jact, f, 0, jnp.where(up_ok, unpack(rim_in[2, 0, f]), 0.0))
            put_shifted(jact, f, rows + 1, jnp.where(down_ok, unpack(rim_in[2, 1, f]), 0.0))

        @alone
        def _():
            up(pairs[slot], 0, 0, 1)
            up(pairs[slot], 1, rows - 1, rows)

    for copy, sends, _ in pending:
        pl.when(sends)(copy.wait_send)
    for slot in sent:
        own_all(slot).wait_send()

    @pl.when(first)
    def _():
        for k in range(2):
            for part in range(3):
                ahead(k, part).wait_send()


def solution(mesh):
    n = mesh.shape["tile"]

    def body(features, g1, s1, k1, b1, g2, s2, k2, b2, uk, ub):
        _, frames, rows, cols, chans = features.shape
        bf16, f32 = jnp.bfloat16, jnp.float32
        hbm = pl.BlockSpec(memory_space=pltpu.HBM)
        vec = lambda v: v.reshape(1, -1)
        dma = pltpu.SemaphoreType.DMA
        made = pl.pallas_call(
            functools.partial(kernel, n),
            out_shape=pltpu.VMEM((frames, 2 * rows, cols, chans), bf16),
            in_specs=[hbm] * 11,
            out_specs=pl.BlockSpec(memory_space=pltpu.VMEM),
            scratch_shapes=[
                pltpu.VMEM((frames + 2, rows, cols, chans), bf16),
                pltpu.VMEM((frames + 2, rows, cols, chans), bf16),
                pltpu.VMEM((frames + 2, rows + 2, cols, KP), bf16),
                pltpu.VMEM((frames + 2, rows + 2, cols, KP), bf16),
                pltpu.VMEM((frames, rows + 2, cols, KP), bf16),
                pltpu.VMEM((9, KP, chans), bf16),
                pltpu.VMEM((9, KP, chans), bf16),
                pltpu.VMEM((2, 2, KP, chans), bf16),
                pltpu.VMEM(uk.shape, bf16),
                pltpu.VMEM((7, 1, chans), f32),
                pltpu.VMEM((1, chans // 2), f32),
                pltpu.VMEM((16, chans), f32),
                pltpu.VMEM((2, 4, chans), f32),
                pltpu.VMEM((2, 4, chans), f32),
                pltpu.VMEM((2 * frames, chans), f32),
                pltpu.VMEM((chans, 128), bf16),
                pltpu.VMEM((128, chans), bf16),
                pltpu.VMEM((3, n, 8, 128), f32),
                pltpu.VMEM((3, 2, frames, cols + cols // 2, 128), bf16),
                pltpu.VMEM((3, 2, frames, cols + cols // 2, 128), bf16),
                pltpu.VMEM((2, 2, 2, cols + cols // 2, 128), bf16),
                pltpu.VMEM((rows + 2, cols + 16, chans), f32),
                dma((11,)),
                dma((5, 2)),
                dma((5, 2)),
                dma((3,)),
                dma((3,)),
                dma((2, 3)),
                dma((2, 3)),
            ],
            compiler_params=pltpu.CompilerParams(
                collective_id=0, has_side_effects=True, vmem_limit_bytes=56 * 1024 * 1024
            ),
        )(
            features[0], vec(g1), vec(s1), k1.reshape(9, 3 * chans, chans), vec(b1),
            vec(g2), vec(s2), k2.reshape(9, 3 * chans, chans), vec(b2), uk, vec(ub),
        )
        return made[None]

    return jax.shard_map(
        body,
        mesh=mesh,
        in_specs=(P(None, "tm", "tile", None, None),) + (P(),) * 10,
        out_specs=P(None, "tm", "tile", None, None),
        check_vma=False,
    )
```

```python
import functools

import jax
import jax.numpy as jnp
from jax import lax
from jax.experimental import pallas as pl
from jax.experimental.pallas import tpu as pltpu
from jax.sharding import PartitionSpec as P

MESH = pl.DeviceIdType.MESH
G = 32
EPS = 1e-06
KP = 640


def split_dot(value, picks):
    m = value.shape[0]
    high = value.astype(jnp.bfloat16).astype(jnp.float32)
    rest = value - high
    mid = rest.astype(jnp.bfloat16).astype(jnp.float32)
    low = rest - mid
    terms = jnp.concatenate([high, mid, low], axis=0).astype(jnp.bfloat16)
    made = jnp.dot(terms, picks, preferred_element_type=jnp.float32)
    return made[0:m] + made[m:2 * m] + made[2 * m:3 * m]


def kernel(
    n,
    feat, g1_h, s1_h, k1, b1_h, g2_h, s2_h, k2, b2_h, uk, ub_h,
    out,
    x_own, h_own, act1, act2, jact, w1, w2, wup, ukv, vecs, ubv, norm, norm_out, norm_in, sums, gmap, smap, stats, rim_out, rim_in, rim_prev, beside,
    loc_sem, row_send, row_recv, own_send, own_recv, prev_send, prev_recv,
):
    frames, rows, cols, chans = feat.shape
    bf16, f32 = jnp.bfloat16, jnp.float32
    tm = lax.axis_index("tm")
    tile = lax.axis_index("tile")
    up_ok = tile > 0
    down_ok = tile < n - 1
    first = tm == 0
    later = tm > 0
    above = lax.rem(tile + n - 1, n)
    below = lax.rem(tile + 1, n)
    per = chans // G
    half = chans // 2
    inverse = 1.0 / float(n * rows * cols * per)
    old = frames - 2
    pairs = ((old, frames), (0, old))

    def local(i, s, d):
        copy = pltpu.make_async_copy(s, d, loc_sem.at[i])
        copy.start()
        return copy

    load_x = local(0, feat, x_own.at[pl.ds(2, frames)])

    far = sorted(range(1, n), key=lambda d: -min(d, n - d))

    barrier = pltpu.get_barrier_semaphore()
    for d in far:
        to = lax.rem(tile + d, n)
        pl.semaphore_signal(barrier, inc=1, device_id=(tm, to), device_id_type=MESH)
    pl.semaphore_signal(barrier, inc=1, device_id=(1 - tm, tile), device_id_type=MESH)

    load_u = local(1, uk, ukv)
    load_v = [
        local(4 + i, ref, vecs.at[i])
        for i, ref in enumerate((g1_h, s1_h, b1_h, g2_h, s2_h, b2_h))
    ]
    load_b = local(10, ub_h, ubv)
    load_1 = local(2, k1, w1.at[:, pl.ds(0, 3 * chans)])

    alone = pl.when(tile >= 0)

    pending = []

    def pack(k, d, f, row):
        low = cols // 2
        side = chans - 128
        rim_out[k, d, f, 0:cols] = row[:, 0:128]
        rim_out[k, d, f, cols:cols + low, 0:side] = row[0:low, 128:chans]
        rim_out[k, d, f, cols:cols + low, 64:64 + side] = row[low:cols, 128:chans]

    def unpack(edge):
        low = cols // 2
        side = chans - 128
        edge = edge.astype(f32)
        rest = jnp.concatenate([edge[cols:cols + low, 0:side], edge[cols:cols + low, 64:64 + side]], axis=0)
        return jnp.concatenate([edge[0:cols], rest], axis=-1)

    def send_rows(k, slot, f0, f1):
        f = pl.ds(f0, f1 - f0)

        def remote(d, who):
            return pltpu.make_async_remote_copy(
                src_ref=rim_out.at[k, d, f], dst_ref=rim_in.at[k, d, f],
                send_sem=row_send.at[slot, d], recv_sem=row_recv.at[slot, d],
                device_id=(tm, who), device_id_type=MESH,
            )

        copies = [(remote(0, below), down_ok, up_ok), (remote(1, above), up_ok, down_ok)]
        for copy, sends, _ in copies:
            pl.when(sends)(copy.start)
        pending.extend(copies)
        return copies

    def wait_rows(copies):
        for copy, _, gets in copies:
            pl.when(gets)(copy.wait_recv)

    sent = []

    def own_copy(slot, d):
        return pltpu.make_async_remote_copy(
            src_ref=stats.at[slot, 0, pl.ds(0, 2)], dst_ref=stats.at[slot, d, pl.ds(0, 2)],
            send_sem=own_send.at[slot], recv_sem=own_recv.at[slot],
            device_id=(tm, lax.rem(tile + d, n)), device_id_type=MESH)

    def own_all(slot):
        view = stats.at[slot, pl.ds(1, n - 1), pl.ds(0, 2)]
        return pltpu.make_async_remote_copy(
            src_ref=view, dst_ref=view, send_sem=own_send.at[slot], recv_sem=own_recv.at[slot],
            device_id=(tm, below), device_id_type=MESH)

    def send_sums(slot):
        for d in range(1, n):
            own_copy(slot, d).start()
        sent.append(slot)

    def ahead(k, part):
        held = feat.at[pl.ds(old, 2)] if k == 0 else h_own.at[pl.ds(frames, 2)]
        source, target = (
            (held, (x_own, h_own)[k].at[pl.ds(0, 2)]),
            (norm_out.at[k], norm_in.at[k]),
            (rim_in.at[k, pl.ds(0, 2), pl.ds(old, 2)], rim_prev.at[k]),
        )[part]
        return pltpu.make_async_remote_copy(
            src_ref=source, dst_ref=target,
            send_sem=prev_send.at[k, part], recv_sem=prev_recv.at[k, part],
            device_id=(1, tile), device_id_type=MESH)

    def give(k, part):
        @pl.when(first)
        def _():
            ahead(k, part).start()

    block_of = lax.broadcasted_iota(jnp.int32, (frames, 128), 1) // G
    block = jnp.where(block_of == lax.broadcasted_iota(jnp.int32, (frames, 128), 0), 1.0, 0.0)

    def put_sums(slot, f0, f1):
        @alone
        def _():
            made = split_dot(sums[...], gmap[...])
            for i in range(2):
                picked = made[i * frames + f0:i * frames + f1] * block[f0:f1]
                stats[slot, 0, i:i + 1] = jnp.sum(picked, axis=0, keepdims=True)

    def add_sums(f, value, fresh):
        for i, v in enumerate((value, value * value)):
            line = slice(i * frames + f, i * frames + f + 1)
            total = jnp.sum(v, axis=0, keepdims=True)
            sums[line] = total if fresh else sums[line] + total

    def norm_from(k, slot, f0, f1, gain):
        @alone
        def _():
            total = jnp.sum(stats[slot, :, 0:2], axis=0)
            spread = jnp.concatenate([total[0:1] * block, total[1:2] * block], axis=0)
            both = split_dot(spread, smap[...]) * inverse
            mean = both[0:frames]
            var = both[frames:2 * frames] - mean * mean
            scale = 0.5 * (lax.rsqrt(var + EPS) * gain)
            norm[f0:f1] = mean[f0:f1]
            norm[8 + f0:8 + f1] = scale[f0:f1]
            if f1 == frames:
                norm_out[k, 0:2] = mean[old:frames]
                norm_out[k, 2:4] = scale[old:frames]

    def put_shifted(dst, f, r, value):
        at = lax.broadcasted_iota(jnp.int32, (cols, 1), 0)
        left = jnp.where(at == 0, 0.0, pltpu.roll(value, 1, 0))
        right = jnp.where(at == cols - 1, 0.0, pltpu.roll(value, cols - 1, 0))
        dst[f, r, :, 0:chans] = left.astype(bf16)
        dst[f, r, :, chans:2 * chans] = value.astype(bf16)
        dst[f, r, :, 2 * chans:3 * chans] = right.astype(bf16)

    def act_row(dst, f, r, value, mean, scale, shift, ok=None):
        scaled = (value - mean) * scale + shift
        made = scaled + scaled * jnp.tanh(scaled)
        if ok is not None:
            made = jnp.where(ok, made, 0.0)
        put_shifted(dst, f, r, made)

    def act_inner(src, dst, f, mean, scale, shift):
        for r in range(rows):
            act_row(dst, f, 1 + r, src[f, r].astype(f32), mean, scale, shift)

    def act_outer(top, bottom, dst, f, mean, scale, shift):
        act_row(dst, f, 0, unpack(top), mean, scale, shift, up_ok)
        act_row(dst, f, rows + 1, unpack(bottom), mean, scale, shift, down_ok)

    inner, outer = tuple(range(1, rows - 1)), (0, rows - 1)

    def lines_of(ref, f0, f1, which, j):
        if which == inner:
            return ref[f0:f1, 1 + j:rows - 1 + j]
        return jnp.concatenate([ref[f0:f1, y + j:y + j + 1] for y in which], axis=1)

    def conv(act, w, pair, which):
        f0, f1 = pair
        m = (f1 - f0) * len(which) * cols
        parts = [
            lines_of(act, f0 + i, f1 + i, which, j).reshape(m, KP) for i in range(3) for j in range(3)
        ]
        return jnp.dot(
            jnp.concatenate(parts, axis=-1), w[...].reshape(9 * KP, chans), preferred_element_type=f32
        )

    lane = lax.broadcasted_iota(jnp.int32, (chans, 128), 1) % G
    chan = lax.broadcasted_iota(jnp.int32, (chans, 128), 0) // per
    gmap[...] = jnp.where(lane == chan, 1.0, 0.0).astype(bf16)
    lane = lax.broadcasted_iota(jnp.int32, (128, chans), 0) % G
    chan = lax.broadcasted_iota(jnp.int32, (128, chans), 1) // per
    smap[...] = jnp.where(lane == chan, 1.0, 0.0).astype(bf16)

    load_x.wait()
    for f in range(frames):
        add_sums(f, x_own[2 + f].reshape(rows * cols, chans).astype(f32), True)
    put_sums(0, 0, frames)
    for f in range(frames):
        pack(0, 0, f, x_own[2 + f, rows - 1])
        pack(0, 1, f, x_own[2 + f, 0])
    pl.semaphore_wait(barrier, n)
    send_sums(0)
    rim_x = send_rows(0, 0, 0, frames)
    give(0, 0)
    load_2 = local(3, k2, w2.at[:, pl.ds(0, 3 * chans)])

    pad = KP - 3 * chans
    beside[:, 0:8] = jnp.zeros((rows + 2, 8, chans), f32)
    beside[:, 8 + cols:16 + cols] = jnp.zeros((rows + 2, 8, chans), f32)
    for act in (act1, act2):
        act[2:2 + frames, :, :, 3 * chans:KP] = jnp.zeros((frames, rows + 2, cols, pad), bf16)
    jact[:, :, :, 3 * chans:KP] = jnp.zeros((frames, rows + 2, cols, pad), bf16)
    w1[:, 3 * chans:KP] = jnp.zeros((9, pad, chans), bf16)
    w2[:, 3 * chans:KP] = jnp.zeros((9, pad, chans), bf16)
    wup[:, :, 3 * chans:KP] = jnp.zeros((2, 2, pad, chans), bf16)

    @pl.when(first)
    def _():
        for act in (act1, act2):
            act[0:2] = jnp.zeros((2, rows + 2, cols, KP), bf16)

    load_u.wait()
    for r in range(2):
        for dy in range(2):
            js = (((0,), (1, 2)) if r == 0 else ((0, 1), (2,)))[dy]
            line = [
                functools.reduce(jnp.add, [ukv[j, k].astype(f32) for j in js]) for k in range(3)
            ]
            zero = jnp.zeros_like(line[0])
            pieces = [(line[0], zero), (line[1] + line[2], line[0] + line[1]), (zero, line[2])]
            for dx, (even, odd) in enumerate(pieces):
                wup[r, dy, dx * chans:(dx + 1) * chans, 0:half] = even.astype(bf16)
                wup[r, dy, dx * chans:(dx + 1) * chans, half:chans] = odd.astype(bf16)
    for copy in load_v:
        copy.wait()
    load_b.wait()
    vecs[6, :, 0:half] = ubv[...]
    vecs[6, :, half:chans] = ubv[...]
    load_1.wait()

    def drain(k):
        for copy, sends, _ in pending:
            pl.when(sends)(copy.wait_send)
        pending.clear()
        for slot in ((0,), (1, 2))[k]:
            own_all(slot).wait_send()

        @pl.when(first)
        def _():
            for part in range(3):
                ahead(k, part).wait_send()

    def stage(k, src, act, gain, shift, rims, piece, after):
        def own(f):
            return norm[f:f + 1], norm[8 + f:9 + f], shift

        def inner_rows(f0, f1):
            for f in range(f0, f1):
                act_inner(src, act, 2 + f, *own(f))

        def outer_rows(f0, f1):
            for f in range(f0, f1):
                act_outer(rim_in[k, 0, f], rim_in[k, 1, f], act, 2 + f, *own(f))

        def take_rims(copies):
            for copy in copies:
                wait_rows(copy)
            give(k, 2)

        if k == 0:
            own_all(0).wait_recv()
            norm_from(0, 0, 0, frames, gain)
            give(0, 1)
            inner_rows(0, frames)
            alone(functools.partial(piece, pairs[0], inner))
            take_rims(rims)
            outer_rows(0, frames)
        else:
            take_rims(rims[0:1])
            own_all(1).wait_recv()
            norm_from(1, 1, *pairs[0], gain)
            give(1, 1)
            inner_rows(*pairs[0])
            outer_rows(*pairs[0])
            wait_rows(rims[1])
            drain(0)
            own_all(2).wait_recv()
            norm_from(1, 2, *pairs[1], gain)
            inner_rows(*pairs[1])
            outer_rows(*pairs[1])
        alone(functools.partial(piece, pairs[0], outer))
        after(0)

        @pl.when(later)
        def _():
            for part in range(3):
                ahead(k, part).wait_recv()
            for f in range(2):
                mean, scale = norm_in[k, f:f + 1], norm_in[k, 2 + f:3 + f]
                act_inner(src, act, f, mean, scale, shift)
                act_outer(rim_prev[k, 0, f], rim_prev[k, 1, f], act, f, mean, scale, shift)

        alone(functools.partial(piece, pairs[1], outer))
        after(1)
        if k == 1:
            alone(functools.partial(piece, pairs[0], inner))
        alone(functools.partial(piece, pairs[1], inner))

    def each(pair, which):
        at = 0
        for f in range(*pair):
            for y in which:
                yield f, y, slice(at * cols, (at + 1) * cols)
                at += 1

    def hidden_piece(pair, which):
        made = (conv(act1, w1, pair, which) + vecs[2]).astype(bf16)
        wide = made.astype(f32)
        m = len(which) * cols
        for f in range(*pair):
            add_sums(f, wide[(f - pair[0]) * m:(f - pair[0] + 1) * m], (which == inner) == (pair == pairs[0]))
        for f, y, at in each(pair, which):
            h_own[2 + f, y] = made[at]
            if y == rows - 1:
                pack(1, 0, f, made[at])
            if y == 0:
                pack(1, 1, f, made[at])

    rim_h, rim_j = [], []

    def hidden_after(slot):
        rim_h.append(send_rows(1, 1 + slot, *pairs[slot]))
        if slot == 0:
            give(1, 0)
            put_sums(1, *pairs[0])
            send_sums(1)

    def joined_piece(pair, which):
        f0, f1 = 2 + pair[0], 2 + pair[1]
        base = lines_of(x_own, f0, f1, which, 0) if which == outer else x_own[f0:f1, 1:rows - 1]
        base = base.reshape(-1, chans).astype(f32)
        made = (base + (conv(act2, w2, pair, which) + vecs[5])).astype(bf16)
        wide = made.astype(f32)
        for f, y, at in each(pair, which):
            if y == rows - 1:
                pack(2, 0, f, made[at])
            if y == 0:
                pack(2, 1, f, made[at])
            put_shifted(jact, f, 1 + y, wide[at])

    def joined_after(slot):
        rim_j.append(send_rows(2, 3 + slot, *pairs[slot]))

    stage(0, x_own, act1, vecs[0], 0.5 * vecs[1], [rim_x], hidden_piece, hidden_after)
    put_sums(2, *pairs[1])
    send_sums(2)
    load_2.wait()
    stage(1, h_own, act2, vecs[3], 0.5 * vecs[4], rim_h, joined_piece, joined_after)

    def up(pair, r, y0, y1):
        f0, f1 = pair
        parts = [
            jact[f0:f1, r + dy + y0:r + dy + y1].reshape((f1 - f0) * (y1 - y0) * cols, KP) for dy in range(2)
        ]
        made = jnp.dot(
            jnp.concatenate(parts, axis=-1), wup[r].reshape(2 * KP, chans), preferred_element_type=f32
        ) + vecs[6]
        made = made.astype(bf16).reshape(f1 - f0, y1 - y0, cols, chans)
        for i in range(f1 - f0):
            for y in range(y0, y1):
                out[f0 + i, 2 * y + r] = made[i, y - y0]

    @alone
    def _():
        up((0, frames), 0, 1, rows)

    @alone
    def _():
        up((0, frames), 1, 0, rows - 1)

    for slot in range(2):
        wait_rows(rim_j[slot])
        for f in range(*pairs[slot]):
            put_shifted(jact, f, 0, jnp.where(up_ok, unpack(rim_in[2, 0, f]), 0.0))
            put_shifted(jact, f, rows + 1, jnp.where(down_ok, unpack(rim_in[2, 1, f]), 0.0))

        @alone
        def _():
            up(pairs[slot], 0, 0, 1)
            up(pairs[slot], 1, rows - 1, rows)

    drain(1)


def solution(mesh):
    n = mesh.shape["tile"]

    def body(features, g1, s1, k1, b1, g2, s2, k2, b2, uk, ub):
        _, frames, rows, cols, chans = features.shape
        bf16, f32 = jnp.bfloat16, jnp.float32
        hbm = pl.BlockSpec(memory_space=pltpu.HBM)
        vec = lambda v: v.reshape(1, -1)
        dma = pltpu.SemaphoreType.DMA
        made = pl.pallas_call(
            functools.partial(kernel, n),
            out_shape=pltpu.VMEM((frames, 2 * rows, cols, chans), bf16),
            in_specs=[hbm] * 11,
            out_specs=pl.BlockSpec(memory_space=pltpu.VMEM),
            scratch_shapes=[
                pltpu.VMEM((frames + 2, rows, cols, chans), bf16),
                pltpu.VMEM((frames + 2, rows, cols, chans), bf16),
                pltpu.VMEM((frames + 2, rows + 2, cols, KP), bf16),
                pltpu.VMEM((frames + 2, rows + 2, cols, KP), bf16),
                pltpu.VMEM((frames, rows + 2, cols, KP), bf16),
                pltpu.VMEM((9, KP, chans), bf16),
                pltpu.VMEM((9, KP, chans), bf16),
                pltpu.VMEM((2, 2, KP, chans), bf16),
                pltpu.VMEM(uk.shape, bf16),
                pltpu.VMEM((7, 1, chans), f32),
                pltpu.VMEM((1, chans // 2), f32),
                pltpu.VMEM((16, chans), f32),
                pltpu.VMEM((2, 4, chans), f32),
                pltpu.VMEM((2, 4, chans), f32),
                pltpu.VMEM((2 * frames, chans), f32),
                pltpu.VMEM((chans, 128), bf16),
                pltpu.VMEM((128, chans), bf16),
                pltpu.VMEM((3, n, 8, 128), f32),
                pltpu.VMEM((3, 2, frames, cols + cols // 2, 128), bf16),
                pltpu.VMEM((3, 2, frames, cols + cols // 2, 128), bf16),
                pltpu.VMEM((2, 2, 2, cols + cols // 2, 128), bf16),
                pltpu.VMEM((rows + 2, cols + 16, chans), f32),
                dma((11,)),
                dma((5, 2)),
                dma((5, 2)),
                dma((3,)),
                dma((3,)),
                dma((2, 3)),
                dma((2, 3)),
            ],
            compiler_params=pltpu.CompilerParams(
                collective_id=0, has_side_effects=True, vmem_limit_bytes=56 * 1024 * 1024
            ),
        )(
            features[0], vec(g1), vec(s1), k1.reshape(9, 3 * chans, chans), vec(b1),
            vec(g2), vec(s2), k2.reshape(9, 3 * chans, chans), vec(b2), uk, vec(ub),
        )
        return made[None]

    return jax.shard_map(
        body,
        mesh=mesh,
        in_specs=(P(None, "tm", "tile", None, None),) + (P(),) * 10,
        out_specs=P(None, "tm", "tile", None, None),
        check_vma=False,
    )
```
